128 devices in a mesh: dp: 8 (over y, core), adapter: 16 (over x, z).
Axes of the slice: x: 4, y: 4, z: 4, core: 2. Of those that a mesh axis runs over, the one named last changes fastest.
Arguments:
- activations: bfloat16 [8192, 28672], P('adapter', 'dp'), may hold values from -6 to 6
- cotangent: bfloat16 [8192, 8192], P('adapter', 'dp'), may hold values from -6 to 6
- factor_in: bfloat16 [512, 16, 28672], P('adapter', None, 'dp'), may hold values from -0.03125 to 0.03125
- factor_out: bfloat16 [512, 16, 8192], P('adapter', None, 'dp'), may hold values from -0.0625 to 0.0625
- adapter_ids: int32 [32, 8], P('adapter'), may hold values from 0 to 511, as said below
- router_weights: float32 [32, 8], P('adapter'), may hold values from 0.25 to 1
Outputs:
- input_grad: float32 [8192, 28672], P('adapter', 'dp')
- grad_factor_in: bfloat16 [512, 16, 28672], P('adapter', None, 'dp')
- grad_factor_out: bfloat16 [512, 16, 8192], P('adapter', None, 'dp')
- router_grad: float32 [32, 8], P('adapter')
The draws below stay inside these ranges and needn't reach their ends.
Inputs may be any that keep to these rules, and one draw needn't show every extreme that they name: `adapter_ids`: the 8 adapters of a request are different. The owner of adapter e is e // 32. Requests are taken in aligned groups of 2 (those of one index of adapter); among the 16 adapters named by one group no owner holds more than 2, and in every group some owner holds exactly 2.
All inputs are finite; a program needn't handle non-finite values.
Results may differ from the reference program's by a relative error of at most 0.012.
Values may be sent and summed in bfloat16 or wider, within the bound.
A program may use at most 128 MiB of HBM per device.

```python
import jax
import jax.numpy as jnp
from jax import lax

D = 8192
FF = 28672
RANK = 16
TOP = 8
REQ_DEV = 2
EXP_DEV = 32
LEN = 256
EXPERTS = 512
REQUESTS = 32
TOKENS = 8192


def draw_adapter_ids(key, part):
    owner_count = EXPERTS // EXP_DEV
    pair_count = REQ_DEV * TOP

    def one_group(group_key):
        keys = jax.random.split(group_key, 4)
        ranked = jax.random.permutation(keys[0], jnp.arange(owner_count, dtype=jnp.int32))
        position = jnp.arange(pair_count, dtype=jnp.int32)
        which = position // 2
        owners = ranked[which]
        base = jax.random.randint(keys[1], (owner_count,), 0, EXP_DEV)
        shifts = jax.random.randint(keys[2], (owner_count,), 1, EXP_DEV)
        local_idx = jnp.where(position % 2 == 0, base[which], (base[which] + shifts[which]) % EXP_DEV)
        chosen = (owners * EXP_DEV + local_idx).astype(jnp.int32)
        order = jax.random.permutation(keys[3], jnp.arange(pair_count, dtype=jnp.int32))
        return chosen[order].reshape(REQ_DEV, TOP).astype(jnp.int32)
    group_keys = jax.random.split(jax.random.fold_in(key, 7), REQUESTS // REQ_DEV)
    return jax.vmap(one_group)(group_keys).reshape(REQUESTS, TOP).astype(jnp.int32)


def levels(rng, dims, cuts, smallest, top_value):
    def one(dim, parts):
        steps = jax.random.uniform(jax.random.fold_in(jax.random.fold_in(rng, 6), dim), (parts,), jnp.float32, smallest / len(cuts), top_value / len(cuts))
        return jnp.repeat(jnp.exp(steps), dims[dim] // parts).reshape((-1,) + (1,) * (len(dims) - dim - 1))

    loudness = one(*cuts[0])
    for cut in cuts[1:]:
        loudness = loudness * one(*cut)
    return loudness


def normal_values(rng, extent, width, most, shards=(), kind=jnp.bfloat16):
    values = jax.random.normal(rng, extent, jnp.float32) * width
    if len(shards) > 0:
        values = levels(rng, extent, shards, -0.22, 0.18) * values
    return jnp.clip(values, min=-most, max=most).astype(kind)


def setup_inputs(seed: int = 0) -> dict:
    key_of = jax.random.split(jax.random.key(seed), 7)
    activations = normal_values(key_of[0], (TOKENS, FF), 1.0, 6.0, ((0, 16), (1, 8)))
    cotangent = normal_values(key_of[1], (TOKENS, D), 1.0, 6.0, ((0, 16), (1, 8)))
    factor_in = normal_values(key_of[2], (EXPERTS, RANK, FF), FF ** -0.5, 0.03125, ((0, 16), (2, 8)))
    factor_out = normal_values(key_of[3], (EXPERTS, RANK, D), D ** -0.5, 0.0625, ((0, 16), (2, 8)))
    adapter_ids = draw_adapter_ids(jax.random.fold_in(key_of[6], 71), 0)
    router_weights = jnp.clip(0.25 + 0.75 * jax.random.uniform(key_of[5], (REQUESTS, TOP), jnp.float32) ** levels(key_of[5], (REQUESTS, TOP), ((0, 16),), -0.2, 0.2), 0.25, 1.0)
    return {"activations": activations, "cotangent": cotangent, "factor_in": factor_in, "factor_out": factor_out, "adapter_ids": adapter_ids, "router_weights": router_weights}


def reference(activations, cotangent, factor_in, factor_out, adapter_ids, router_weights):
    def one_request(item):
        rows_in, rows_out, picks, mixing = item
        inputs32 = rows_in.astype(jnp.float32)
        outputs32 = rows_out.astype(jnp.float32)
        picked_in = factor_in[picks].astype(jnp.float32)
        picked_out = factor_out[picks].astype(jnp.float32)
        projected = jnp.einsum("lf,krf->lkr", inputs32, picked_in)
        pulled = jnp.einsum("ld,krd->lkr", outputs32, picked_out)
        router_row = jnp.sum(projected * pulled, axis=(0, 2))
        pulled_weighted = (mixing[None, :, None] * pulled).astype(jnp.bfloat16)
        projected_weighted = (mixing[None, :, None] * projected).astype(jnp.bfloat16)
        input_rows = jnp.einsum("lkr,krf->lf", pulled_weighted.astype(jnp.float32), picked_in)
        term_in = jnp.einsum("lkr,lf->krf", pulled_weighted.astype(jnp.float32), inputs32).astype(jnp.bfloat16)
        term_out = jnp.einsum("lkr,ld->krd", projected_weighted.astype(jnp.float32), outputs32).astype(jnp.bfloat16)
        return input_rows, term_in, term_out, router_row

    input_rows, term_in, term_out, router_grad = lax.map(
        one_request,
        (activations.reshape(REQUESTS, LEN, FF), cotangent.reshape(REQUESTS, LEN, D), adapter_ids, router_weights))
    flat_ids = adapter_ids.reshape(REQUESTS * TOP)
    grad_factor_in = jax.ops.segment_sum(term_in.reshape(REQUESTS * TOP, RANK, FF).astype(jnp.float32), flat_ids, num_segments=EXPERTS).astype(jnp.bfloat16)
    grad_factor_out = jax.ops.segment_sum(term_out.reshape(REQUESTS * TOP, RANK, D).astype(jnp.float32), flat_ids, num_segments=EXPERTS).astype(jnp.bfloat16)
    input_grad = input_rows.reshape(TOKENS, FF)
    return input_grad, grad_factor_in, grad_factor_out, router_grad
```

```python
import functools

import jax
import jax.numpy as jnp
from jax import lax
from jax.experimental import pallas as pl
from jax.experimental.pallas import tpu as pltpu
from jax.sharding import PartitionSpec as P

MESH = pl.DeviceIdType.MESH
SIDE = 4
OWNERS = SIDE * SIDE
CAP = 2
RANK = 16
EXP_DEV = 32
DP = 8
ORDER = (
    (1, 1), (3, 3), (1, 3), (3, 1), (2, 0), (0, 2), (2, 2), (2, 1),
    (1, 2), (2, 3), (3, 2), (1, 0), (3, 0), (0, 1), (0, 3),
)


def rot(off):
    return off[0] * SIDE + off[1]


def exchange_kernel(
    slot_of_pair, pair_of_slot,
    tab_ref, scale_ref, fi_hbm, fo_hbm, act_hbm, cot_hbm,
    ret_in, ret_out, pair_in_hbm, pw_out, tab_out, router_out,
    fi, fo, act, cot, send_in, send_out, got_in, got_out, pair_in, pair_out,
    term_in, term_out, back_in, back_out, tab, tab_smem,
    rs_send, rs_got, kept, ag, rp,
    load_sem, out_sem, tab_ss, tab_rs, fo_ss, fo_rs, fi_ss, fi_rs,
    bi_ss, bi_rs, bo_ss, bo_rs, rs_ss, rs_rs, ag_ss, ag_rs, rp_ss, rp_rs,
):
    me = lax.axis_index("adapter")
    mx, mz = me // SIDE, me % SIDE
    dp = lax.axis_index("dp")

    def there(off):
        return {"adapter": ((mx + off[0]) % SIDE) * SIDE + (mz + off[1]) % SIDE}

    def back(off):
        return {"adapter": ((mx + SIDE - off[0]) % SIDE) * SIDE + (mz + SIDE - off[1]) % SIDE}

    def beside(d):
        return {"dp": (dp + d) % DP}

    loads = []
    for i, (src, dst) in enumerate(((fo_hbm, fo), (fi_hbm, fi), (cot_hbm, cot), (act_hbm, act))):
        loads.append(pltpu.make_async_copy(src, dst, load_sem.at[i]))
        loads[-1].start()

    bar = pltpu.get_barrier_semaphore()
    for off in ORDER:
        pl.semaphore_signal(bar, inc=1, device_id=there(off), device_id_type=MESH)
    for d in range(1, DP):
        pl.semaphore_signal(bar, inc=1, device_id=beside(d), device_id_type=MESH)
    pl.semaphore_wait(bar, len(ORDER) + DP - 1)

    def push(src, dst, ss, rs, dev):
        c = pltpu.make_async_remote_copy(
            src_ref=src, dst_ref=dst, send_sem=ss, recv_sem=rs, device_id=dev, device_id_type=MESH
        )
        c.start()
        return c

    tabs = []
    for i, off in enumerate(ORDER):
        j = rot(off)
        tabs.append(push(tab_ref.at[j], tab.at[j], tab_ss.at[i], tab_rs.at[i], back(off)))
    tab[0] = tab_ref[0]
    for c in tabs:
        c.wait()
    local = pltpu.make_async_copy(tab, tab_smem, out_sem.at[0])
    local.start()
    local.wait()

    def pick(src, dst, j, c):
        dst[j * CAP + c] = src[jnp.clip(tab_smem[j, 0, c], 0, EXP_DEV - 1)]

    loads[0].wait()
    fos = []
    for i, off in enumerate(ORDER):
        j = rot(off)
        for c in range(CAP):
            pick(fo, send_out, j, c)
        rows = pl.ds(j * CAP, CAP)
        fos.append(push(send_out.at[rows], got_out.at[rows], fo_ss.at[i], fo_rs.at[i], there(off)))
    for c in range(CAP):
        pick(fo, got_out, 0, c)

    loads[1].wait()
    fis = []
    for c in range(CAP):
        for i, off in enumerate(ORDER):
            j = rot(off)
            pick(fi, send_in, j, c)
            n = c * len(ORDER) + i
            rows = pl.ds(j * CAP + c, 1)
            fis.append(push(send_in.at[rows], got_in.at[rows], fi_ss.at[n], fi_rs.at[n], there(off)))
    for c in range(CAP):
        pick(fi, got_in, 0, c)

    def combine(step):
        cs = []
        for d in range(1, DP):
            cs.append(push(rs_send.at[step, (dp + d) % DP], rs_got.at[step, d],
                           rs_ss.at[step, d], rs_rs.at[step, d], beside(d)))
        total = rs_send[step, dp]
        for c in cs:
            c.wait()
        for d in range(1, DP):
            total = total + rs_got[step, d]
        return total

    def spread(step, total):
        scale = scale_ref[pl.ds(dp // (DP // 2), 1), :]
        ag[step, dp] = (total * scale).astype(jnp.bfloat16)
        return [
            push(ag.at[step, dp], ag.at[step, dp], ag_ss.at[step, d], ag_rs.at[step, d], beside(d))
            for d in range(1, DP)
        ]

    half = DP // 2
    length = act.shape[1]
    top = slot_of_pair.shape[0] // 2
    width = top * RANK
    chunk = length // half

    def project(step, rows, got, pair):
        for b in range(2):
            for k in range(top):
                p = b * top + k
                pair[p] = got[slot_of_pair[p]]
            part = lax.dot_general(
                rows[b], pair[b * top:(b + 1) * top].reshape(width, pair.shape[2]),
                (((1,), (1,)), ((), ())), preferred_element_type=jnp.float32,
            )
            for h in range(half):
                rs_send[step, b * half + h] = part[h * chunk:(h + 1) * chunk]

    def terms(step, rows, term, cols):
        n = rows.shape[2]
        for b in range(2):
            w = ag[step, b * half:(b + 1) * half].reshape(length, width)
            for s in range(0, n, cols):
                t = lax.dot_general(
                    w, rows[b, :, s:s + cols], (((0,), (0,)), ((), ())),
                    preferred_element_type=jnp.float32,
                )
                term[b * top:(b + 1) * top, :, s:s + cols] = t.astype(jnp.bfloat16).reshape(top, RANK, cols)

    for c in fos:
        c.wait()
    loads[2].wait()
    project(0, cot, got_out, pair_out)
    pulled = combine(0)
    kept[...] = pulled
    ags = spread(0, pulled)
    loads[3].wait()
    for c in ags:
        c.wait()

    terms(0, act, term_in, 512)
    bis = []
    for c in range(CAP):
        for i, off in enumerate(ORDER):
            j = rot(off)
            s = j * CAP + c
            back_in[s] = term_in[pair_of_slot[s]]
            n = c * len(ORDER) + i
            rows = pl.ds(s, 1)
            bis.append(push(back_in.at[rows], ret_in.at[rows], bi_ss.at[n], bi_rs.at[n], back(off)))
    for c in range(CAP):
        back_in[c] = term_in[pair_of_slot[c]]
    own = [pltpu.make_async_copy(back_in.at[pl.ds(0, CAP)], ret_in.at[pl.ds(0, CAP)], out_sem.at[0])]
    own[0].start()

    for c in fis:
        c.wait()
    project(1, act, got_in, pair_in)
    own.append(pltpu.make_async_copy(pair_in, pair_in_hbm, out_sem.at[1]))
    own[1].start()
    projected = combine(1)
    ags = spread(1, projected)
    rp[dp] = jnp.broadcast_to(jnp.sum(projected * kept[...], axis=0, keepdims=True), rp.shape[1:])
    rps = [
        push(rp.at[dp], rp.at[dp], rp_ss.at[d], rp_rs.at[d], beside(d)) for d in range(1, DP)
    ]
    for c in ags:
        c.wait()
    terms(1, cot, term_out, 512)
    bos = []
    for i, off in enumerate(ORDER):
        j = rot(off)
        for c in range(CAP):
            back_out[j * CAP + c] = term_out[pair_of_slot[j * CAP + c]]
        rows = pl.ds(j * CAP, CAP)
        bos.append(push(back_out.at[rows], ret_out.at[rows], bo_ss.at[i], bo_rs.at[i], back(off)))
    for c in range(CAP):
        back_out[c] = term_out[pair_of_slot[c]]
    own.append(pltpu.make_async_copy(back_out.at[pl.ds(0, CAP)], ret_out.at[pl.ds(0, CAP)], out_sem.at[2]))
    own[2].start()

    pw_out[...] = ag[0]
    tab_out[...] = tab[...]
    for c in rps:
        c.wait()
    for b in range(2):
        acc = rp[b * half]
        for h in range(1, half):
            acc = acc + rp[b * half + h]
        router_out[b] = acc
    for c in own + bis + bos:
        c.wait()


def finish_kernel(tab, pw, pair_in, ret_in, ret_out, ig, gi, go, place):
    rows = place.shape[0]

    @pl.when(pl.program_id(0) == 0)
    def _():
        r = lax.broadcasted_iota(jnp.int32, (RANK, rows), 0)
        col = lax.broadcasted_iota(jnp.int32, (RANK, rows), 1)
        for s in range(OWNERS * CAP):
            hit = (tab[s // CAP, 0, s % CAP] * RANK + r) == col
            place[s * RANK:(s + 1) * RANK, :] = jnp.where(hit, 1.0, 0.0).astype(jnp.bfloat16)
        go[...] = lax.dot_general(
            place[...], ret_out[...], (((0,), (0,)), ((), ())), preferred_element_type=jnp.float32
        ).astype(jnp.bfloat16)

    gi[...] = lax.dot_general(
        place[...], ret_in[...], (((0,), (0,)), ((), ())), preferred_element_type=jnp.float32
    ).astype(jnp.bfloat16)
    for b in range(2):
        ig[b] = jnp.dot(pw[b], pair_in[b], preferred_element_type=jnp.float32)


def body(activations, cotangent, factor_in, factor_out, adapter_ids, router_weights):
    req, top = adapter_ids.shape
    tokens, ff = activations.shape
    model = cotangent.shape[1]
    length = tokens // req
    pairs = req * top
    slots = OWNERS * CAP
    chunk = tokens // DP
    width = top * RANK
    bf, f32, i32 = jnp.bfloat16, jnp.float32, jnp.int32

    me = lax.axis_index("adapter")
    ids = adapter_ids.reshape(pairs)
    owner = ids // EXP_DEV
    before = jnp.arange(pairs)[:, None] > jnp.arange(pairs)[None, :]
    nth = jnp.sum((owner[:, None] == owner[None, :]) & before, axis=1)
    turn = ((me // SIDE - owner // SIDE) % SIDE) * SIDE + (me - owner) % SIDE
    slot_of_pair = jnp.minimum(turn * CAP + nth, slots - 1).astype(i32)
    hits = slot_of_pair[None, :] == jnp.arange(slots)[:, None]
    pair_of_slot = jnp.max(jnp.where(hits, jnp.arange(pairs)[None, :], 0), axis=1).astype(i32)
    named = jnp.max(jnp.where(hits, (ids % EXP_DEV)[None, :], -1), axis=1).astype(i32)
    tab = jnp.pad(named.reshape(OWNERS, 1, CAP), ((0, 0), (0, 0), (0, 128 - CAP)))
    scale = jnp.repeat(router_weights, RANK, axis=1)

    any_ = pl.BlockSpec(memory_space=pl.ANY)
    smem = pl.BlockSpec(memory_space=pltpu.SMEM)
    vmem = pl.BlockSpec(memory_space=pltpu.VMEM)
    dma = pltpu.SemaphoreType.DMA
    far = OWNERS - 1
    ret_in, ret_out, pair_in, pw, tab_all, router = pl.pallas_call(
        exchange_kernel,
        out_shape=(
            jax.ShapeDtypeStruct((slots, RANK, ff), bf),
            jax.ShapeDtypeStruct((slots, RANK, model), bf),
            jax.ShapeDtypeStruct((pairs, RANK, ff), bf),
            jax.ShapeDtypeStruct((DP, chunk, width), bf),
            jax.ShapeDtypeStruct((OWNERS, 1, 128), i32),
            jax.ShapeDtypeStruct((req, 8, width), f32),
        ),
        in_specs=[smem, smem, vmem, vmem, any_, any_, any_, any_],
        out_specs=(any_, any_, any_, vmem, vmem, vmem),
        scratch_shapes=[
            pltpu.VMEM((EXP_DEV, RANK, ff), bf),
            pltpu.VMEM((EXP_DEV, RANK, model), bf),
            pltpu.VMEM((req, length, ff), bf),
            pltpu.VMEM((req, length, model), bf),
            pltpu.VMEM((slots, RANK, ff), bf),
            pltpu.VMEM((slots, RANK, model), bf),
            pltpu.VMEM((slots, RANK, ff), bf),
            pltpu.VMEM((slots, RANK, model), bf),
            pltpu.VMEM((pairs, RANK, ff), bf),
            pltpu.VMEM((pairs, RANK, model), bf),
            pltpu.VMEM((pairs, RANK, ff), bf),
            pltpu.VMEM((pairs, RANK, model), bf),
            pltpu.VMEM((slots, RANK, ff), bf),
            pltpu.VMEM((slots, RANK, model), bf),
            pltpu.VMEM((OWNERS, 1, 128), i32),
            pltpu.SMEM((OWNERS, 1, 128), i32),
            pltpu.VMEM((2, DP, chunk, width), f32),
            pltpu.VMEM((2, DP, chunk, width), f32),
            pltpu.VMEM((chunk, width), f32),
            pltpu.VMEM((2, DP, chunk, width), bf),
            pltpu.VMEM((DP, 8, width), f32),
            dma((4,)), dma((3,)),
            dma((far,)), dma((far,)),
            dma((far,)), dma((far,)),
            dma((CAP * far,)), dma((CAP * far,)),
            dma((CAP * far,)), dma((CAP * far,)),
            dma((far,)), dma((far,)),
            dma((2, DP)), dma((2, DP)), dma((2, DP)), dma((2, DP)), dma((DP,)), dma((DP,)),
        ],
        compiler_params=pltpu.CompilerParams(
            collective_id=0, has_side_effects=True, vmem_limit_bytes=48 << 20
        ),
        name="exchange",
    )(
        slot_of_pair, pair_of_slot, tab, scale, factor_in, factor_out,
        activations.reshape(req, length, ff), cotangent.reshape(req, length, model),
    )

    cols = 512
    rows = slots * RANK
    input_grad, grad_in, grad_out = pl.pallas_call(
        finish_kernel,
        grid=(ff // cols,),
        out_shape=(
            jax.ShapeDtypeStruct((req, length, ff), f32),
            jax.ShapeDtypeStruct((EXP_DEV * RANK, ff), bf),
            jax.ShapeDtypeStruct((EXP_DEV * RANK, model), bf),
        ),
        in_specs=[
            smem,
            pl.BlockSpec((req, length, width), lambda i: (0, 0, 0)),
            pl.BlockSpec((req, width, cols), lambda i: (0, 0, i)),
            pl.BlockSpec((rows, cols), lambda i: (0, i)),
            pl.BlockSpec((rows, model), lambda i: (0, 0)),
        ],
        out_specs=(
            pl.BlockSpec((req, length, cols), lambda i: (0, 0, i)),
            pl.BlockSpec((EXP_DEV * RANK, cols), lambda i: (0, i)),
            pl.BlockSpec((EXP_DEV * RANK, model), lambda i: (0, 0)),
        ),
        scratch_shapes=[pltpu.VMEM((rows, EXP_DEV * RANK), bf)],
        compiler_params=pltpu.CompilerParams(vmem_limit_bytes=32 << 20),
        name="finish",
    )(
        tab_all, pw.reshape(req, length, width), pair_in.reshape(req, width, ff),
        ret_in.reshape(rows, ff), ret_out.reshape(rows, model),
    )
    router_grad = jnp.sum(router[:, 0, :].reshape(req, top, RANK), axis=2)
    return (
        input_grad.reshape(tokens, ff),
        grad_in.reshape(EXP_DEV, RANK, ff),
        grad_out.reshape(EXP_DEV, RANK, model),
        router_grad,
    )


def solution(mesh):
    return jax.shard_map(
        body,
        mesh=mesh,
        in_specs=(
            P("adapter", "dp"),
            P("adapter", "dp"),
            P("adapter", None, "dp"),
            P("adapter", None, "dp"),
            P("adapter", None),
            P("adapter", None),
        ),
        out_specs=(
            P("adapter", "dp"),
            P("adapter", None, "dp"),
            P("adapter", None, "dp"),
            P("adapter", None),
        ),
        check_vma=False,
    )
```

```python
import jax
import jax.numpy as jnp
from jax import lax
from jax.experimental import pallas as pl
from jax.experimental.pallas import tpu as pltpu
from jax.sharding import PartitionSpec as P

MESH = pl.DeviceIdType.MESH
SIDE = 4
OWNERS = SIDE * SIDE
CAP = 2
RANK = 16
EXP_DEV = 32
DP = 8
HALF = DP // 2
LANES = 128
COLS = 512
FINAL = 256
PARTS = 2
ORDER = (
    (1, 1), (3, 3), (1, 3), (3, 1), (2, 0), (0, 2), (2, 2), (2, 1),
    (1, 2), (2, 3), (3, 2), (1, 0), (3, 0), (0, 1), (0, 3),
)
BF, F32, I32 = jnp.bfloat16, jnp.float32, jnp.int32


def rot(off):
    return off[0] * SIDE + off[1]


def exchange_kernel(
    ids, weights, fi_hbm, fo_hbm, act_hbm, cot_hbm,
    ig, gi, go, router,
    fi, fo, act, cot, send_in, send_out, got_in, got_out, pair_in, pair_out,
    term_in, term_out, back_in, back_out, ret_in, ret_out, place,
    tab_send, tab, tab_smem, inv, inv_smem, slot_of_pair,
    rs_send, rs_got, kept, ag, rp,
    load_sem, tab_sem, tab_ss, tab_rs, fo_ss, fo_rs, fi_ss, fi_rs,
    bi_ss, bi_rs, bo_ss, bo_rs, rs_ss, rs_rs, ag_ss, ag_rs, rp_ss, rp_rs,
):
    me = lax.axis_index("adapter")
    mx, mz = me // SIDE, me % SIDE
    dp = lax.axis_index("dp")
    top = ids.shape[1]
    pairs = 2 * top
    width = top * RANK
    length = act.shape[1]
    chunk = length // HALF

    def there(off):
        return {"adapter": ((mx + off[0]) % SIDE) * SIDE + (mz + off[1]) % SIDE}

    def back(off):
        return {"adapter": ((mx + SIDE - off[0]) % SIDE) * SIDE + (mz + SIDE - off[1]) % SIDE}

    def beside(d):
        return {"dp": (dp + d) % DP}

    def push(src, dst, ss, rs, dev):
        c = pltpu.make_async_remote_copy(
            src_ref=src, dst_ref=dst, send_sem=ss, recv_sem=rs, device_id=dev, device_id_type=MESH
        )
        c.start()
        return c

    bar = pltpu.get_barrier_semaphore()
    for off in ORDER:
        pl.semaphore_signal(bar, inc=1, device_id=there(off), device_id_type=MESH)
    for d in range(1, DP):
        pl.semaphore_signal(bar, inc=1, device_id=beside(d), device_id_type=MESH)

    loads = []
    for i, (src, dst) in enumerate(((fo_hbm, fo), (fi_hbm, fi), (cot_hbm, cot), (act_hbm, act))):
        loads.append(pltpu.make_async_copy(src, dst, load_sem.at[i]))
        loads[-1].start()

    row = lax.broadcasted_iota(I32, (OWNERS, LANES), 0)
    lane = lax.broadcasted_iota(I32, (OWNERS, LANES), 1)
    owner = []
    named = jnp.full((OWNERS, LANES), -1, I32)
    which = jnp.zeros((OWNERS, LANES), I32)
    for p in range(pairs):
        e = ids[p // top, p % top]
        o = lax.shift_right_logical(e, 5)
        nth = jnp.int32(0)
        for q in owner:
            nth = nth + jnp.where(q == o, 1, 0)
        owner.append(o)
        nth = jnp.minimum(nth, CAP - 1)
        turn = ((mx - lax.shift_right_logical(o, 2)) & 3) * SIDE + ((mz - o) & 3)
        slot_of_pair[p] = turn * CAP + nth
        hit = (row == turn) & (lane == nth)
        named = jnp.where(hit, e & (EXP_DEV - 1), named)
        which = jnp.where(hit, p, which)
    tab_send[...] = named
    inv[...] = which
    inv_copy = pltpu.make_async_copy(inv, inv_smem, tab_sem.at[1])
    inv_copy.start()

    pl.semaphore_wait(bar, len(ORDER) + DP - 1)
    tabs = []
    for i, off in enumerate(ORDER):
        at = pl.ds(rot(off), 1)
        tabs.append(push(tab_send.at[at], tab.at[at], tab_ss.at[i], tab_rs.at[i], back(off)))
    tab[0:1] = tab_send[0:1]
    for c in tabs:
        c.wait()
    tab_copy = pltpu.make_async_copy(tab, tab_smem, tab_sem.at[0])
    tab_copy.start()
    loads[0].wait()
    loads[1].wait()
    tab_copy.wait()

    def pick(src, dst, j, c):
        dst[j, c] = src[jnp.clip(tab_smem[j, c], 0, EXP_DEV - 1)]

    fos, fis = [], []
    for i, off in enumerate(ORDER):
        j = rot(off)
        for c in range(CAP):
            pick(fo, send_out, j, c)
        fos.append(push(send_out.at[j], got_out.at[j], fo_ss.at[i], fo_rs.at[i], there(off)))
    for c in range(CAP):
        pick(fo, got_out, 0, c)
    for c in range(CAP):
        for i, off in enumerate(ORDER):
            j = rot(off)
            pick(fi, send_in, j, c)
            n = c * len(ORDER) + i
            fis.append(push(send_in.at[j, c], got_in.at[j, c], fi_ss.at[n], fi_rs.at[n], there(off)))
    for c in range(CAP):
        pick(fi, got_in, 0, c)

    def project(step, rows, got, pair):
        for b in range(2):
            for k in range(top):
                p = b * top + k
                s = slot_of_pair[p]
                pair[p] = got[lax.shift_right_logical(s, 1), s & (CAP - 1)]
            part = lax.dot_general(
                rows[b], pair[b * top:(b + 1) * top].reshape(width, pair.shape[2]),
                (((1,), (1,)), ((), ())), preferred_element_type=F32,
            )
            for h in range(HALF):
                rs_send[step, b * HALF + h] = part[h * chunk:(h + 1) * chunk]

    def combine(step):
        cs = [
            push(rs_send.at[step, (dp + d) % DP], rs_got.at[step, d],
                 rs_ss.at[step, d], rs_rs.at[step, d], beside(d))
            for d in range(1, DP)
        ]
        total = rs_send[step, dp]
        for d in range(1, DP):
            cs[d - 1].wait()
            total = total + rs_got[step, d]
        return total

    group = lax.shift_right_logical(lax.broadcasted_iota(I32, (1, width), 1), 4)
    scale = jnp.zeros((1, width), F32)
    for k in range(top):
        scale = jnp.where(group == k, weights[dp // HALF, k], scale)

    def spread(step, total):
        ag[step, dp] = (total * scale).astype(BF)
        return [
            push(ag.at[step, dp], ag.at[step, dp], ag_ss.at[step, d], ag_rs.at[step, d], beside(d))
            for d in range(1, DP)
        ]

    def terms(step, rows, term):
        for b in range(2):
            w = ag[step, b * HALF:(b + 1) * HALF].reshape(length, width)
            for s in range(0, rows.shape[2], COLS):
                t = lax.dot_general(
                    w, rows[b, :, s:s + COLS], (((0,), (0,)), ((), ())), preferred_element_type=F32
                )
                term[b * top:(b + 1) * top, :, s:s + COLS] = t.astype(BF).reshape(top, RANK, COLS)

    loads[2].wait()
    loads[3].wait()
    inv_copy.wait()
    for c in fos:
        c.wait()
    project(0, cot, got_out, pair_out)
    pulled = combine(0)
    kept[...] = pulled
    for c in spread(0, pulled):
        c.wait()

    def give(term, out, ret, ss, rs, part, parts):
        n = term.shape[2] // parts
        at = pl.ds(part * n, n)
        cs = []
        for i, off in enumerate(ORDER):
            j = rot(off)
            for c in range(CAP):
                out[j, c, :, at] = term[inv_smem[j, c], :, at]
            k = part * len(ORDER) + i
            cs.append(push(out.at[j, :, :, at], ret.at[j, :, :, at], ss.at[k], rs.at[k], back(off)))
        for c in range(CAP):
            ret[0, c, :, at] = term[inv_smem[0, c], :, at]
        return cs

    terms(0, act, term_in)
    bis = [give(term_in, back_in, ret_in, bi_ss, bi_rs, part, PARTS) for part in range(PARTS)]

    for c in fis:
        c.wait()
    project(1, act, got_in, pair_in)
    projected = combine(1)
    ags = spread(1, projected)
    rp[dp] = jnp.broadcast_to(jnp.sum(projected * kept[...], axis=0, keepdims=True), rp.shape[1:])
    rps = [push(rp.at[dp], rp.at[dp], rp_ss.at[d], rp_rs.at[d], beside(d)) for d in range(1, DP)]
    for c in ags:
        c.wait()
    terms(1, cot, term_out)
    bos = give(term_out, back_out, ret_out, bo_ss, bo_rs, 0, 1)

    for b in range(2):
        w = ag[0, b * HALF:(b + 1) * HALF].reshape(length, width)
        f = pair_in.at[b * top:(b + 1) * top]
        for s in range(0, fi.shape[2], COLS):
            ig[b, :, s:s + COLS] = jnp.dot(
                w, f[:, :, s:s + COLS].reshape(width, COLS), preferred_element_type=F32
            )
    for c in rps:
        c.wait()
    sums = jnp.concatenate(
        [jnp.sum(rp[b * HALF:(b + 1) * HALF], axis=0)[0:1] for b in range(2)]
        + [jnp.zeros((6, width), F32)], axis=0,
    )
    fold = jnp.where(
        lax.shift_right_logical(lax.broadcasted_iota(I32, (width, LANES), 0), 4)
        == lax.broadcasted_iota(I32, (width, LANES), 1), 1.0, 0.0,
    )
    router[...] = jnp.dot(
        sums, fold, precision=lax.Precision.HIGHEST, preferred_element_type=F32
    )[0:2, 0:top]

    total_rows = EXP_DEV * RANK
    slots = OWNERS * CAP
    spot = lax.broadcasted_iota(I32, (1, slots * RANK), 1)
    target = jnp.full((1, slots * RANK), -1, I32)
    for s in range(slots):
        e = tab_smem[s // CAP, s % CAP]
        target = jnp.where(lax.shift_right_logical(spot, 4) == s, e * RANK + (spot & (RANK - 1)), target)
    for r in range(0, total_rows, LANES):
        at = lax.broadcasted_iota(I32, (LANES, slots * RANK), 0) + r
        place[r:r + LANES, :] = jnp.where(at == target, 1.0, 0.0).astype(BF)

    def settle(ret, grad, start, stop):
        for s in range(start, stop, FINAL):
            total = jnp.dot(
                place[...], ret[:, :, :, s:s + FINAL].reshape(slots * RANK, FINAL), preferred_element_type=F32
            )
            grad[:, :, s:s + FINAL] = total.astype(BF).reshape(EXP_DEV, RANK, FINAL)

    ff = fi.shape[2]
    for part in range(PARTS):
        for c in bis[part]:
            c.wait()
        settle(ret_in, gi, part * ff // PARTS, (part + 1) * ff // PARTS)
    for c in bos:
        c.wait()
    settle(ret_out, go, 0, fo.shape[2])


def body(activations, cotangent, factor_in, factor_out, adapter_ids, router_weights):
    req, top = adapter_ids.shape
    tokens, ff = activations.shape
    model = cotangent.shape[1]
    length = tokens // req
    pairs = req * top
    chunk = tokens // DP
    width = top * RANK
    hbm = pl.BlockSpec(memory_space=pltpu.HBM)
    smem = pl.BlockSpec(memory_space=pltpu.SMEM)
    vmem = pl.BlockSpec(memory_space=pltpu.VMEM)
    dma = pltpu.SemaphoreType.DMA
    far = OWNERS - 1

    def slots(n):
        return pltpu.VMEM((OWNERS, CAP, RANK, n), BF)

    def by_pair(n):
        return pltpu.VMEM((pairs, RANK, n), BF)

    input_grad, grad_in, grad_out, router_grad = pl.pallas_call(
        exchange_kernel,
        out_shape=(
            pltpu.VMEM((req, length, ff), F32),
            pltpu.VMEM((EXP_DEV, RANK, ff), BF),
            pltpu.VMEM((EXP_DEV, RANK, model), BF),
            pltpu.VMEM((req, top), F32),
        ),
        in_specs=[smem, smem, hbm, hbm, hbm, hbm],
        out_specs=(vmem, vmem, vmem, vmem),
        scratch_shapes=[
            pltpu.VMEM((EXP_DEV, RANK, ff), BF),
            pltpu.VMEM((EXP_DEV, RANK, model), BF),
            pltpu.VMEM((req, length, ff), BF),
            pltpu.VMEM((req, length, model), BF),
            slots(ff), slots(model), slots(ff), slots(model),
            by_pair(ff), by_pair(model), by_pair(ff), by_pair(model),
            slots(ff), slots(model), slots(ff), slots(model),
            pltpu.VMEM((EXP_DEV * RANK, OWNERS * CAP * RANK), BF),
            pltpu.VMEM((OWNERS, LANES), I32),
            pltpu.VMEM((OWNERS, LANES), I32),
            pltpu.SMEM((OWNERS, LANES), I32),
            pltpu.VMEM((OWNERS, LANES), I32),
            pltpu.SMEM((OWNERS, LANES), I32),
            pltpu.SMEM((pairs,), I32),
            pltpu.VMEM((2, DP, chunk, width), F32),
            pltpu.VMEM((2, DP, chunk, width), F32),
            pltpu.VMEM((chunk, width), F32),
            pltpu.VMEM((2, DP, chunk, width), BF),
            pltpu.VMEM((DP, 8, width), F32),
            dma((4,)), dma((2,)),
            dma((far,)), dma((far,)),
            dma((far,)), dma((far,)),
            dma((CAP * far,)), dma((CAP * far,)),
            dma((PARTS * far,)), dma((PARTS * far,)),
            dma((far,)), dma((far,)),
            dma((2, DP)), dma((2, DP)), dma((2, DP)), dma((2, DP)), dma((DP,)), dma((DP,)),
        ],
        compiler_params=pltpu.CompilerParams(
            collective_id=0, has_side_effects=True, vmem_limit_bytes=44 << 20
        ),
        name="exchange",
    )(
        adapter_ids,
        router_weights,
        *(
            pltpu.with_memory_space_constraint(x, pltpu.HBM)
            for x in (
                factor_in, factor_out,
                activations.reshape(req, length, ff), cotangent.reshape(req, length, model),
            )
        ),
    )
    return input_grad.reshape(tokens, ff), grad_in, grad_out, router_grad


def solution(mesh):
    return jax.shard_map(
        body,
        mesh=mesh,
        in_specs=(
            P("adapter", "dp"),
            P("adapter", "dp"),
            P("adapter", None, "dp"),
            P("adapter", None, "dp"),
            P("adapter", None),
            P("adapter", None),
        ),
        out_specs=(
            P("adapter", "dp"),
            P("adapter", None, "dp"),
            P("adapter", None, "dp"),
            P("adapter", None),
        ),
        check_vma=False,
    )
```

```python
import jax
import jax.numpy as jnp
from jax import lax
from jax.experimental import pallas as pl
from jax.experimental.pallas import tpu as pltpu
from jax.sharding import PartitionSpec as P

MESH = pl.DeviceIdType.MESH
SIDE = 4
OWNERS = SIDE * SIDE
CAP = 2
RANK = 16
EXP_DEV = 32
DP = 8
HALF = DP // 2
LANES = 128
COLS = 512
FINAL = 256
PARTS = 2
SPLIT = 4
ORDER = (
    (1, 1), (3, 3), (1, 3), (3, 1), (2, 0), (0, 2), (2, 2), (2, 1),
    (1, 2), (2, 3), (3, 2), (1, 0), (3, 0), (0, 1), (0, 3),
)
BF, F32, I32 = jnp.bfloat16, jnp.float32, jnp.int32


def rot(off):
    return off[0] * SIDE + off[1]


def exchange_kernel(
    ids, weights, fi_hbm, fo_hbm, act_hbm, cot_hbm,
    ig, gi, go, router,
    fi, fo, act, cot, send_in, send_out, got_in, got_out, pair_in, pair_out,
    term_in, term_out, back_in, back_out, ret_in, ret_out, place,
    tab_send, tab, tab_smem, inv, inv_smem, slot_of_pair,
    rs_send, rs_got, kept, ag, rp,
    load_sem, tab_sem, tab_ss, tab_rs, fo_ss, fo_rs, fi_ss, fi_rs,
    bi_ss, bi_rs, bo_ss, bo_rs, rs_ss, rs_rs, ag_ss, ag_rs, rp_ss, rp_rs,
):
    me = lax.axis_index("adapter")
    mx, mz = me // SIDE, me % SIDE
    dp = lax.axis_index("dp")
    top = ids.shape[1]
    pairs = 2 * top
    width = top * RANK
    length = act.shape[1]
    chunk = length // HALF

    def there(off):
        return {"adapter": ((mx + off[0]) % SIDE) * SIDE + (mz + off[1]) % SIDE}

    def back(off):
        return {"adapter": ((mx + SIDE - off[0]) % SIDE) * SIDE + (mz + SIDE - off[1]) % SIDE}

    def beside(d):
        return {"dp": (dp + d) % DP}

    def push(src, dst, ss, rs, dev):
        c = pltpu.make_async_remote_copy(
            src_ref=src, dst_ref=dst, send_sem=ss, recv_sem=rs, device_id=dev, device_id_type=MESH
        )
        c.start()
        return c

    bar = pltpu.get_barrier_semaphore()
    for off in ORDER:
        pl.semaphore_signal(bar, inc=1, device_id=there(off), device_id_type=MESH)
    for d in range(1, DP):
        pl.semaphore_signal(bar, inc=1, device_id=beside(d), device_id_type=MESH)

    loads = []
    for i, (src, dst) in enumerate(((fo_hbm, fo), (fi_hbm, fi), (cot_hbm, cot), (act_hbm, act))):
        loads.append(pltpu.make_async_copy(src, dst, load_sem.at[i]))
        loads[-1].start()

    row = lax.broadcasted_iota(I32, (OWNERS, LANES), 0)
    lane = lax.broadcasted_iota(I32, (OWNERS, LANES), 1)
    owner = []
    named = jnp.full((OWNERS, LANES), -1, I32)
    which = jnp.zeros((OWNERS, LANES), I32)
    for p in range(pairs):
        e = ids[p // top, p % top]
        o = lax.shift_right_logical(e, 5)
        nth = jnp.int32(0)
        for q in owner:
            nth = nth + jnp.where(q == o, 1, 0)
        owner.append(o)
        nth = jnp.minimum(nth, CAP - 1)
        turn = ((mx - lax.shift_right_logical(o, 2)) & 3) * SIDE + ((mz - o) & 3)
        slot_of_pair[p] = turn * CAP + nth
        hit = (row == turn) & (lane == nth)
        named = jnp.where(hit, e & (EXP_DEV - 1), named)
        which = jnp.where(hit, p, which)
    tab_send[...] = named
    inv[...] = which
    inv_copy = pltpu.make_async_copy(inv, inv_smem, tab_sem.at[1])
    inv_copy.start()

    pl.semaphore_wait(bar, len(ORDER) + DP - 1)
    tabs = []
    for i, off in enumerate(ORDER):
        at = pl.ds(rot(off), 1)
        tabs.append(push(tab_send.at[at], tab.at[at], tab_ss.at[i], tab_rs.at[i], back(off)))
    tab[0:1] = tab_send[0:1]
    for c in tabs:
        c.wait()
    tab_copy = pltpu.make_async_copy(tab, tab_smem, tab_sem.at[0])
    tab_copy.start()
    loads[0].wait()
    loads[1].wait()
    tab_copy.wait()

    def pick(src, dst, j, c):
        dst[j, c] = src[jnp.clip(tab_smem[j, c], 0, EXP_DEV - 1)]

    fos, fis = [], []
    for i, off in enumerate(ORDER):
        j = rot(off)
        for c in range(CAP):
            pick(fo, send_out, j, c)
        fos.append(push(send_out.at[j], got_out.at[j], fo_ss.at[i], fo_rs.at[i], there(off)))
    for c in range(CAP):
        pick(fo, got_out, 0, c)
    for c in range(CAP):
        for i, off in enumerate(ORDER):
            j = rot(off)
            pick(fi, send_in, j, c)
            n = c * len(ORDER) + i
            fis.append(push(send_in.at[j, c], got_in.at[j, c], fi_ss.at[n], fi_rs.at[n], there(off)))
    for c in range(CAP):
        pick(fi, got_in, 0, c)

    def project(step, rows, got, pair):
        for b in range(2):
            for k in range(top):
                p = b * top + k
                s = slot_of_pair[p]
                pair[p] = got[lax.shift_right_logical(s, 1), s & (CAP - 1)]
            part = lax.dot_general(
                rows[b], pair[b * top:(b + 1) * top].reshape(width, pair.shape[2]),
                (((1,), (1,)), ((), ())), preferred_element_type=F32,
            )
            for h in range(HALF):
                rs_send[step, b * HALF + h] = part[h * chunk:(h + 1) * chunk]

    def combine(step):
        cs = [
            push(rs_send.at[step, (dp + d) % DP], rs_got.at[step, d],
                 rs_ss.at[step, d], rs_rs.at[step, d], beside(d))
            for d in range(1, DP)
        ]
        total = rs_send[step, dp]
        for d in range(1, DP):
            cs[d - 1].wait()
            total = total + rs_got[step, d]
        return total

    group = lax.shift_right_logical(lax.broadcasted_iota(I32, (1, width), 1), 4)
    scale = jnp.zeros((1, width), F32)
    for k in range(top):
        scale = jnp.where(group == k, weights[dp // HALF, k], scale)

    def spread(step, total):
        ag[step, dp] = (total * scale).astype(BF)
        return [
            push(ag.at[step, dp], ag.at[step, dp], ag_ss.at[step, d], ag_rs.at[step, d], beside(d))
            for d in range(1, DP)
        ]

    def terms(step, rows, term):
        for b in range(2):
            w = ag[step, b * HALF:(b + 1) * HALF].reshape(length, width)
            for s in range(0, rows.shape[2], COLS):
                t = lax.dot_general(
                    w, rows[b, :, s:s + COLS], (((0,), (0,)), ((), ())), preferred_element_type=F32
                )
                term[b * top:(b + 1) * top, :, s:s + COLS] = t.astype(BF).reshape(top, RANK, COLS)

    loads[2].wait()
    loads[3].wait()
    inv_copy.wait()
    for c in fos:
        c.wait()
    project(0, cot, got_out, pair_out)
    pulled = combine(0)
    kept[...] = pulled
    for c in spread(0, pulled):
        c.wait()

    def give(term, out, ret, ss, rs, part, parts):
        n = term.shape[2] // parts
        at = pl.ds(part * n, n)
        cs = []
        for i, off in enumerate(ORDER):
            j = rot(off)
            for c in range(CAP):
                out[j, c, :, at] = term[inv_smem[j, c], :, at]
            k = part * len(ORDER) + i
            cs.append(push(out.at[j, :, :, at], ret.at[j, :, :, at], ss.at[k], rs.at[k], back(off)))
        for c in range(CAP):
            ret[0, c, :, at] = term[inv_smem[0, c], :, at]
        return cs

    terms(0, act, term_in)
    bis = [give(term_in, back_in, ret_in, bi_ss, bi_rs, part, PARTS) for part in range(PARTS)]

    for c in fis:
        c.wait()
    project(1, act, got_in, pair_in)
    projected = combine(1)
    ags = spread(1, projected)
    rp[dp] = jnp.broadcast_to(jnp.sum(projected * kept[...], axis=0, keepdims=True), rp.shape[1:])
    rps = [push(rp.at[dp], rp.at[dp], rp_ss.at[d], rp_rs.at[d], beside(d)) for d in range(1, DP)]
    for c in ags:
        c.wait()
    terms(1, cot, term_out)
    bos = give(term_out, back_out, ret_out, bo_ss, bo_rs, 0, 1)

    for b in range(2):
        w = ag[0, b * HALF:(b + 1) * HALF].reshape(length, width)
        f = pair_in.at[b * top:(b + 1) * top]
        for s in range(0, fi.shape[2], COLS):
            ig[b, :, s:s + COLS] = jnp.dot(
                w, f[:, :, s:s + COLS].reshape(width, COLS), preferred_element_type=F32
            )
    for c in rps:
        c.wait()
    sums = jnp.concatenate(
        [jnp.sum(rp[b * HALF:(b + 1) * HALF], axis=0)[0:1] for b in range(2)]
        + [jnp.zeros((6, width), F32)], axis=0,
    )
    fold = jnp.where(
        lax.shift_right_logical(lax.broadcasted_iota(I32, (width, LANES), 0), 4)
        == lax.broadcasted_iota(I32, (width, LANES), 1), 1.0, 0.0,
    )
    router[...] = jnp.dot(
        sums, fold, precision=lax.Precision.HIGHEST, preferred_element_type=F32
    )[0:2, 0:top]

    total_rows = EXP_DEV * RANK
    slots = OWNERS * CAP
    spot = lax.broadcasted_iota(I32, (1, slots * RANK), 1)
    target = jnp.full((1, slots * RANK), -1, I32)
    for s in range(slots):
        e = tab_smem[s // CAP, s % CAP]
        target = jnp.where(lax.shift_right_logical(spot, 4) == s, e * RANK + (spot & (RANK - 1)), target)
    for r in range(0, total_rows, LANES):
        at = lax.broadcasted_iota(I32, (LANES, slots * RANK), 0) + r
        place[r:r + LANES, :] = jnp.where(at == target, 1.0, 0.0).astype(BF)

    def settle(ret, grad, start, stop, step):
        for s in range(start, stop, step):
            total = jnp.dot(
                place[...], ret[:, :, :, s:s + step].reshape(slots * RANK, step), preferred_element_type=F32
            )
            grad[:, :, s:s + step] = total.astype(BF).reshape(EXP_DEV, RANK, step)

    ff = fi.shape[2]
    for part in range(PARTS):
        for c in bis[part]:
            c.wait()
        settle(ret_in, gi, part * ff // PARTS, (part + 1) * ff // PARTS, FINAL)
    for c in bos:
        c.wait()
    settle(ret_out, go, 0, fo.shape[2], 256)


def store_kernel(*refs):
    n = len(refs) // 2
    srcs, dsts, sem = refs[:n], refs[n:2 * n], refs[-1]
    copies = []
    for src, dst in zip(srcs, dsts):
        parts = SPLIT if src.shape[0] % SPLIT == 0 else 1
        step = src.shape[0] // parts
        for p in range(parts):
            at = pl.ds(p * step, step)
            copies.append(pltpu.make_async_copy(src.at[at], dst.at[at], sem.at[len(copies)]))
    for c in copies:
        c.start()
    for c in copies:
        c.wait()


def body(activations, cotangent, factor_in, factor_out, adapter_ids, router_weights):
    req, top = adapter_ids.shape
    tokens, ff = activations.shape
    model = cotangent.shape[1]
    length = tokens // req
    pairs = req * top
    chunk = tokens // DP
    width = top * RANK
    hbm = pl.BlockSpec(memory_space=pltpu.HBM)
    smem = pl.BlockSpec(memory_space=pltpu.SMEM)
    vmem = pl.BlockSpec(memory_space=pltpu.VMEM)
    dma = pltpu.SemaphoreType.DMA
    far = OWNERS - 1

    def slots(n):
        return pltpu.VMEM((OWNERS, CAP, RANK, n), BF)

    def by_pair(n):
        return pltpu.VMEM((pairs, RANK, n), BF)

    results = pl.pallas_call(
        exchange_kernel,
        out_shape=(
            pltpu.VMEM((req, length, ff), F32),
            pltpu.VMEM((EXP_DEV, RANK, ff), BF),
            pltpu.VMEM((EXP_DEV, RANK, model), BF),
            pltpu.VMEM((req, top), F32),
        ),
        in_specs=[smem, smem, hbm, hbm, hbm, hbm],
        out_specs=(vmem, vmem, vmem, vmem),
        scratch_shapes=[
            pltpu.VMEM((EXP_DEV, RANK, ff), BF),
            pltpu.VMEM((EXP_DEV, RANK, model), BF),
            pltpu.VMEM((req, length, ff), BF),
            pltpu.VMEM((req, length, model), BF),
            slots(ff), slots(model), slots(ff), slots(model),
            by_pair(ff), by_pair(model), by_pair(ff), by_pair(model),
            slots(ff), slots(model), slots(ff), slots(model),
            pltpu.VMEM((EXP_DEV * RANK, OWNERS * CAP * RANK), BF),
            pltpu.VMEM((OWNERS, LANES), I32),
            pltpu.VMEM((OWNERS, LANES), I32),
            pltpu.SMEM((OWNERS, LANES), I32),
            pltpu.VMEM((OWNERS, LANES), I32),
            pltpu.SMEM((OWNERS, LANES), I32),
            pltpu.SMEM((pairs,), I32),
            pltpu.VMEM((2, DP, chunk, width), F32),
            pltpu.VMEM((2, DP, chunk, width), F32),
            pltpu.VMEM((chunk, width), F32),
            pltpu.VMEM((2, DP, chunk, width), BF),
            pltpu.VMEM((DP, 8, width), F32),
            dma((4,)), dma((2,)),
            dma((far,)), dma((far,)),
            dma((far,)), dma((far,)),
            dma((CAP * far,)), dma((CAP * far,)),
            dma((PARTS * far,)), dma((PARTS * far,)),
            dma((far,)), dma((far,)),
            dma((2, DP)), dma((2, DP)), dma((2, DP)), dma((2, DP)), dma((DP,)), dma((DP,)),
        ],
        compiler_params=pltpu.CompilerParams(
            collective_id=0, has_side_effects=True, vmem_limit_bytes=44 << 20
        ),
        name="exchange",
    )(
        adapter_ids,
        router_weights,
        *(
            pltpu.with_memory_space_constraint(x, pltpu.HBM)
            for x in (
                factor_in, factor_out,
                activations.reshape(req, length, ff), cotangent.reshape(req, length, model),
            )
        ),
    )
    input_grad, grad_in, grad_out, router_grad = pl.pallas_call(
        store_kernel,
        out_shape=tuple(jax.ShapeDtypeStruct(r.shape, r.dtype) for r in results),
        in_specs=[vmem] * 4,
        out_specs=(hbm,) * 4,
        scratch_shapes=[dma((4 * SPLIT,))],
        compiler_params=pltpu.CompilerParams(vmem_limit_bytes=1 << 20),
        name="store",
    )(*(pltpu.with_memory_space_constraint(r, pltpu.VMEM) for r in results))
    return input_grad.reshape(tokens, ff), grad_in, grad_out, router_grad


def solution(mesh):
    return jax.shard_map(
        body,
        mesh=mesh,
        in_specs=(
            P("adapter", "dp"),
            P("adapter", "dp"),
            P("adapter", None, "dp"),
            P("adapter", None, "dp"),
            P("adapter", None),
            P("adapter", None),
        ),
        out_specs=(
            P("adapter", "dp"),
            P("adapter", None, "dp"),
            P("adapter", None, "dp"),
            P("adapter", None),
        ),
        check_vma=False,
    )
```

```python
import jax
import jax.numpy as jnp
from jax import lax
from jax.experimental import pallas as pl
from jax.experimental.pallas import tpu as pltpu
from jax.sharding import PartitionSpec as P

MESH = pl.DeviceIdType.MESH
SIDE = 4
OWNERS = SIDE * SIDE
CAP = 2
RANK = 16
EXP_DEV = 32
DP = 8
HALF = DP // 2
LANES = 128
COLS = 512
FINAL = 256
PARTS = 2
SPLIT = 1
ORDER = ((2, 0), (0, 2), (1, 0), (3, 0), (0, 1), (0, 3), (1, 1), (3, 3), (1, 3), (3, 1), (2, 1), (2, 3), (1, 2), (3, 2), (2, 2))
ORDER_FO = ((2, 0), (0, 2), (1, 0), (3, 0), (0, 1), (0, 3), (1, 1), (3, 3), (1, 3), (3, 1), (2, 1), (2, 3), (1, 2), (3, 2), (2, 2))
ORDER_FI = ((2, 0), (0, 2), (1, 0), (3, 0), (0, 1), (0, 3), (1, 1), (3, 3), (1, 3), (3, 1), (2, 1), (2, 3), (1, 2), (3, 2), (2, 2))
ORDER_BI = ((2, 0), (0, 2), (1, 0), (3, 0), (0, 1), (0, 3), (1, 1), (3, 3), (1, 3), (3, 1), (2, 1), (2, 3), (1, 2), (3, 2), (2, 2))
ORDER_BO = ((2, 2), (2, 1), (2, 3), (1, 2), (3, 2), (1, 1), (3, 3), (1, 3), (3, 1), (2, 0), (0, 2), (1, 0), (3, 0), (0, 1), (0, 3))
BF, F32, I32 = jnp.bfloat16, jnp.float32, jnp.int32


def rot(off):
    return off[0] * SIDE + off[1]


def exchange_kernel(
    ids_hbm, weights_hbm, fi_hbm, fo_hbm, act_hbm, cot_hbm,
    ig, gi, go, router,
    fi, fo, act, cot, send_in, send_out, got_in, got_out, pair_in, pair_out,
    term_in, term_out, back_in, back_out, ret_in, ret_out, place,
    ids, weights, tab_send, tab_got, tab, inv, inv_smem, slot_of_pair,
    rs_send, rs_got, kept, ag, rp,
    load_sem, tab_sem, tab_ss, tab_rs, fo_ss, fo_rs, fi_ss, fi_rs,
    bi_ss, bi_rs, bo_ss, bo_rs, rs_ss, rs_rs, ag_ss, ag_rs, rp_ss, rp_rs,
):
    me = lax.axis_index("adapter")
    mx, mz = me // SIDE, me % SIDE
    dp = lax.axis_index("dp")
    top = ids.shape[1]
    pairs = 2 * top
    width = top * RANK
    length = act.shape[1]
    chunk = length // HALF

    def there(off):
        return {"adapter": ((mx + off[0]) % SIDE) * SIDE + (mz + off[1]) % SIDE}

    def back(off):
        return {"adapter": ((mx + SIDE - off[0]) % SIDE) * SIDE + (mz + SIDE - off[1]) % SIDE}

    def beside(d):
        return {"dp": (dp + d) % DP}

    def push(src, dst, ss, rs, dev):
        c = pltpu.make_async_remote_copy(
            src_ref=src, dst_ref=dst, send_sem=ss, recv_sem=rs, device_id=dev, device_id_type=MESH
        )
        c.start()
        return c

    loads = []
    for i, (src, dst) in enumerate(((fo_hbm, fo), (fi_hbm, fi), (cot_hbm, cot), (act_hbm, act))):
        loads.append(pltpu.make_async_copy(src, dst, load_sem.at[i]))
    id_copies = [
        pltpu.make_async_copy(ids_hbm, ids, tab_sem.at[2]),
        pltpu.make_async_copy(weights_hbm, weights, tab_sem.at[3]),
    ]
    for c in id_copies:
        c.start()
    bar = pltpu.get_barrier_semaphore()
    for off in ORDER:
        pl.semaphore_signal(bar, inc=1, device_id=there(off), device_id_type=MESH)
    for d in range(1, DP):
        pl.semaphore_signal(bar, inc=1, device_id=beside(d), device_id_type=MESH)
    for c in loads:
        c.start()

    def turn_of(p):
        o = lax.shift_right_logical(ids[p // top, p % top], 5)
        return ((mx - lax.shift_right_logical(o, 2)) & 3) * SIDE + ((mz - o) & 3)

    row = lax.broadcasted_iota(I32, (OWNERS, LANES), 0)
    lane = lax.broadcasted_iota(I32, (OWNERS, LANES), 1)
    named = jnp.full((OWNERS, LANES), -1, I32)
    which = jnp.zeros((OWNERS, LANES), I32)
    held = jnp.zeros((OWNERS, LANES), I32)
    id_copies[0].wait()
    for p in range(pairs):
        mine = row == turn_of(p)
        hit = mine & (lane == held)
        named = jnp.where(hit, ids[p // top, p % top] & (EXP_DEV - 1), named)
        which = jnp.where(hit, p, which)
        held = jnp.where(mine, held + 1, held)
    tab_send[...] = named

    pl.semaphore_wait(bar, len(ORDER) + DP - 1)
    tabs = []
    for i, off in enumerate(ORDER):
        at = pl.ds(rot(off), 1)
        tabs.append(push(tab_send.at[at], tab_got.at[at], tab_ss.at[i], tab_rs.at[i], back(off)))
    tab_got[0:1] = named[0:1]
    inv[...] = which
    inv_copy = pltpu.make_async_copy(inv, inv_smem, tab_sem.at[1])
    inv_copy.start()

    def pick(src, dst, j, c):
        dst[j, c] = src[jnp.clip(tab[j, c], 0, EXP_DEV - 1)]

    fos, fis = [], []
    loads[0].wait()
    for c in tabs:
        c.wait_recv()
    tab_copy = pltpu.make_async_copy(tab_got, tab, tab_sem.at[0])
    tab_copy.start()
    tab_copy.wait()
    for i, off in enumerate(ORDER_FO):
        j = rot(off)
        for c in range(CAP):
            pick(fo, send_out, j, c)
        fos.append(push(send_out.at[j], got_out.at[j], fo_ss.at[i], fo_rs.at[i], there(off)))
    for c in range(CAP):
        pick(fo, got_out, 0, c)
    loads[1].wait()
    for c in range(CAP):
        for i, off in enumerate(ORDER_FI):
            j = rot(off)
            pick(fi, send_in, j, c)
            n = c * len(ORDER) + i
            fis.append(push(send_in.at[j, c], got_in.at[j, c], fi_ss.at[n], fi_rs.at[n], there(off)))
    for c in range(CAP):
        pick(fi, got_in, 0, c)
    for c in tabs:
        c.wait_send()
    turns = []
    for p in range(pairs):
        nth = jnp.int32(0)
        t = turn_of(p)
        for q in turns:
            nth = nth + jnp.where(q == t, 1, 0)
        turns.append(t)
        slot_of_pair[p] = t * CAP + jnp.minimum(nth, CAP - 1)
    id_copies[1].wait()

    def project(step, rows, got, pair):
        for b in range(2):
            for k in range(top):
                p = b * top + k
                s = slot_of_pair[p]
                pair[p] = got[lax.shift_right_logical(s, 1), s & (CAP - 1)]
            part = lax.dot_general(
                rows[b], pair[b * top:(b + 1) * top].reshape(width, pair.shape[2]),
                (((1,), (1,)), ((), ())), preferred_element_type=F32,
            )
            for h in range(HALF):
                rs_send[step, b * HALF + h] = part[h * chunk:(h + 1) * chunk]

    def combine(step):
        cs = [
            push(rs_send.at[step, (dp + d) % DP], rs_got.at[step, d],
                 rs_ss.at[step, d], rs_rs.at[step, d], beside(d))
            for d in range(1, DP)
        ]
        total = rs_send[step, dp]
        for d in range(1, DP):
            cs[d - 1].wait()
            total = total + rs_got[step, d]
        return total

    group = lax.shift_right_logical(lax.broadcasted_iota(I32, (1, width), 1), 4)
    scale = jnp.zeros((1, width), F32)
    for k in range(top):
        scale = jnp.where(group == k, weights[dp // HALF, k], scale)

    def spread(step, total):
        ag[step, dp] = (total * scale).astype(BF)
        return [
            push(ag.at[step, dp], ag.at[step, dp], ag_ss.at[step, d], ag_rs.at[step, d], beside(d))
            for d in range(1, DP)
        ]

    def terms(step, rows, term):
        for b in range(2):
            w = ag[step, b * HALF:(b + 1) * HALF].reshape(length, width)
            for s in range(0, rows.shape[2], COLS):
                t = lax.dot_general(
                    w, rows[b, :, s:s + COLS], (((0,), (0,)), ((), ())), preferred_element_type=F32
                )
                term[b * top:(b + 1) * top, :, s:s + COLS] = t.astype(BF).reshape(top, RANK, COLS)

    loads[2].wait()
    loads[3].wait()
    inv_copy.wait()
    for c in fos:
        c.wait()
    project(0, cot, got_out, pair_out)
    pulled = combine(0)
    kept[...] = pulled
    for c in spread(0, pulled):
        c.wait()

    def give(order, term, out, ret, ss, rs, part, parts):
        n = term.shape[2] // parts
        at = pl.ds(part * n, n)
        cs = []
        for i, off in enumerate(order):
            j = rot(off)
            for c in range(CAP):
                out[j, c, :, at] = term[inv_smem[j, c], :, at]
            k = part * len(ORDER) + i
            cs.append(push(out.at[j, :, :, at], ret.at[j, :, :, at], ss.at[k], rs.at[k], back(off)))
        for c in range(CAP):
            ret[0, c, :, at] = term[inv_smem[0, c], :, at]
        return cs

    terms(0, act, term_in)
    bis = [give(ORDER_BI, term_in, back_in, ret_in, bi_ss, bi_rs, part, PARTS) for part in range(PARTS)]

    for c in fis:
        c.wait()
    project(1, act, got_in, pair_in)
    projected = combine(1)
    ags = spread(1, projected)
    rp[dp] = jnp.broadcast_to(jnp.sum(projected * kept[...], axis=0, keepdims=True), rp.shape[1:])
    rps = [push(rp.at[dp], rp.at[dp], rp_ss.at[d], rp_rs.at[d], beside(d)) for d in range(1, DP)]
    for c in ags:
        c.wait()
    terms(1, cot, term_out)
    bos = give(ORDER_BO, term_out, back_out, ret_out, bo_ss, bo_rs, 0, 1)

    for b in range(2):
        w = ag[0, b * HALF:(b + 1) * HALF].reshape(length, width)
        f = pair_in.at[b * top:(b + 1) * top]
        for s in range(0, fi.shape[2], COLS):
            ig[b, :, s:s + COLS] = jnp.dot(
                w, f[:, :, s:s + COLS].reshape(width, COLS), preferred_element_type=F32
            )
    for c in rps:
        c.wait()
    sums = jnp.concatenate(
        [jnp.sum(rp[b * HALF:(b + 1) * HALF], axis=0)[0:1] for b in range(2)]
        + [jnp.zeros((6, width), F32)], axis=0,
    )
    fold = jnp.where(
        lax.shift_right_logical(lax.broadcasted_iota(I32, (width, LANES), 0), 4)
        == lax.broadcasted_iota(I32, (width, LANES), 1), 1.0, 0.0,
    )
    router[...] = jnp.dot(
        sums, fold, precision=lax.Precision.HIGHEST, preferred_element_type=F32
    )[0:2, 0:top]

    total_rows = EXP_DEV * RANK
    slots = OWNERS * CAP
    spot = lax.broadcasted_iota(I32, (1, slots * RANK), 1)
    target = jnp.full((1, slots * RANK), -1, I32)
    for s in range(slots):
        e = tab[s // CAP, s % CAP]
        target = jnp.where(lax.shift_right_logical(spot, 4) == s, e * RANK + (spot & (RANK - 1)), target)
    for r in range(0, total_rows, LANES):
        at = lax.broadcasted_iota(I32, (LANES, slots * RANK), 0) + r
        place[r:r + LANES, :] = jnp.where(at == target, 1.0, 0.0).astype(BF)

    def settle(ret, grad, start, stop, step):
        for s in range(start, stop, step):
            total = jnp.dot(
                place[...], ret[:, :, :, s:s + step].reshape(slots * RANK, step), preferred_element_type=F32
            )
            grad[:, :, s:s + step] = total.astype(BF).reshape(EXP_DEV, RANK, step)

    ff = fi.shape[2]
    for part in range(PARTS):
        for c in bis[part]:
            c.wait()
        settle(ret_in, gi, part * ff // PARTS, (part + 1) * ff // PARTS, FINAL)
    for c in bos:
        c.wait()
    settle(ret_out, go, 0, fo.shape[2], 256)


def store_kernel(*refs):
    n = len(refs) // 2
    srcs, dsts, sem = refs[:n], refs[n:2 * n], refs[-1]
    copies = []
    for src, dst in zip(srcs, dsts):
        parts = SPLIT if src.shape[0] % SPLIT == 0 else 1
        step = src.shape[0] // parts
        for p in range(parts):
            at = pl.ds(p * step, step)
            copies.append(pltpu.make_async_copy(src.at[at], dst.at[at], sem.at[len(copies)]))
    for c in copies:
        c.start()
    for c in copies:
        c.wait()


def body(activations, cotangent, factor_in, factor_out, adapter_ids, router_weights):
    req, top = adapter_ids.shape
    tokens, ff = activations.shape
    model = cotangent.shape[1]
    length = tokens // req
    pairs = req * top
    chunk = tokens // DP
    width = top * RANK
    hbm = pl.BlockSpec(memory_space=pltpu.HBM)
    vmem = pl.BlockSpec(memory_space=pltpu.VMEM)
    dma = pltpu.SemaphoreType.DMA
    far = OWNERS - 1

    def slots(n):
        return pltpu.VMEM((OWNERS, CAP, RANK, n), BF)

    def by_pair(n):
        return pltpu.VMEM((pairs, RANK, n), BF)

    results = pl.pallas_call(
        exchange_kernel,
        out_shape=(
            pltpu.VMEM((req, length, ff), F32),
            pltpu.VMEM((EXP_DEV, RANK, ff), BF),
            pltpu.VMEM((EXP_DEV, RANK, model), BF),
            pltpu.VMEM((req, top), F32),
        ),
        in_specs=[hbm] * 6,
        out_specs=(vmem, vmem, vmem, vmem),
        scratch_shapes=[
            pltpu.VMEM((EXP_DEV, RANK, ff), BF),
            pltpu.VMEM((EXP_DEV, RANK, model), BF),
            pltpu.VMEM((req, length, ff), BF),
            pltpu.VMEM((req, length, model), BF),
            slots(ff), slots(model), slots(ff), slots(model),
            by_pair(ff), by_pair(model), by_pair(ff), by_pair(model),
            slots(ff), slots(model), slots(ff), slots(model),
            pltpu.VMEM((EXP_DEV * RANK, OWNERS * CAP * RANK), BF),
            pltpu.SMEM((req, top), I32),
            pltpu.SMEM((req, top), F32),
            pltpu.VMEM((OWNERS, LANES), I32),
            pltpu.VMEM((OWNERS, LANES), I32),
            pltpu.SMEM((OWNERS, LANES), I32),
            pltpu.VMEM((OWNERS, LANES), I32),
            pltpu.SMEM((OWNERS, LANES), I32),
            pltpu.SMEM((pairs,), I32),
            pltpu.VMEM((2, DP, chunk, width), F32),
            pltpu.VMEM((2, DP, chunk, width), F32),
            pltpu.VMEM((chunk, width), F32),
            pltpu.VMEM((2, DP, chunk, width), BF),
            pltpu.VMEM((DP, 8, width), F32),
            dma((4,)), dma((4,)),
            dma((far,)), dma((far,)),
            dma((far,)), dma((far,)),
            dma((CAP * far,)), dma((CAP * far,)),
            dma((PARTS * far,)), dma((PARTS * far,)),
            dma((far,)), dma((far,)),
            dma((2, DP)), dma((2, DP)), dma((2, DP)), dma((2, DP)), dma((DP,)), dma((DP,)),
        ],
        compiler_params=pltpu.CompilerParams(
            collective_id=0, has_side_effects=True, vmem_limit_bytes=44 << 20
        ),
        name="exchange",
    )(
        *(
            pltpu.with_memory_space_constraint(x, pltpu.HBM)
            for x in (
                adapter_ids, router_weights, factor_in, factor_out,
                activations.reshape(req, length, ff), cotangent.reshape(req, length, model),
            )
        ),
    )
    input_grad, grad_in, grad_out, router_grad = pl.pallas_call(
        store_kernel,
        out_shape=tuple(jax.ShapeDtypeStruct(r.shape, r.dtype) for r in results),
        in_specs=[vmem] * 4,
        out_specs=(hbm,) * 4,
        scratch_shapes=[dma((4 * SPLIT,))],
        compiler_params=pltpu.CompilerParams(vmem_limit_bytes=1 << 20),
        name="store",
    )(*(pltpu.with_memory_space_constraint(r, pltpu.VMEM) for r in results))
    return input_grad.reshape(tokens, ff), grad_in, grad_out, router_grad


def solution(mesh):
    return jax.shard_map(
        body,
        mesh=mesh,
        in_specs=(
            P("adapter", "dp"),
            P("adapter", "dp"),
            P("adapter", None, "dp"),
            P("adapter", None, "dp"),
            P("adapter", None),
            P("adapter", None),
        ),
        out_specs=(
            P("adapter", "dp"),
            P("adapter", None, "dp"),
            P("adapter", None, "dp"),
            P("adapter", None),
        ),
        check_vma=False,
    )
```

```python
import jax
import jax.numpy as jnp
from jax import lax
from jax.experimental import pallas as pl
from jax.experimental.pallas import tpu as pltpu
from jax.sharding import PartitionSpec as P

MESH = pl.DeviceIdType.MESH
SIDE = 4
OWNERS = SIDE * SIDE
CAP = 2
RANK = 16
EXP_DEV = 32
DP = 8
HALF = DP // 2
LANES = 128
COLS = 512
FINAL = 256
PARTS = 2
SPLIT = 1
ORDER = ((2, 0), (0, 2), (1, 0), (3, 0), (0, 1), (0, 3), (1, 1), (3, 3), (1, 3), (3, 1), (2, 1), (2, 3), (1, 2), (3, 2), (2, 2))
ORDER_FO = ((2, 0), (0, 2), (1, 0), (3, 0), (0, 1), (0, 3), (1, 1), (3, 3), (1, 3), (3, 1), (2, 1), (2, 3), (1, 2), (3, 2), (2, 2))
ORDER_FI = ((2, 0), (0, 2), (1, 0), (3, 0), (0, 1), (0, 3), (1, 1), (3, 3), (1, 3), (3, 1), (2, 1), (2, 3), (1, 2), (3, 2), (2, 2))
ORDER_BI = ((2, 0), (0, 2), (1, 0), (3, 0), (0, 1), (0, 3), (1, 1), (3, 3), (1, 3), (3, 1), (2, 1), (2, 3), (1, 2), (3, 2), (2, 2))
ORDER_BO = ((2, 2), (2, 1), (2, 3), (1, 2), (3, 2), (1, 1), (3, 3), (1, 3), (3, 1), (2, 0), (0, 2), (1, 0), (3, 0), (0, 1), (0, 3))
BF, F32, I32 = jnp.bfloat16, jnp.float32, jnp.int32


def rot(off):
    return off[0] * SIDE + off[1]


def exchange_kernel(
    ids_hbm, weights_hbm, fi_hbm, fo_hbm, act_hbm, cot_hbm,
    ig, gi, go, router,
    fi, fo, act, cot, send_in, send_out, got_in, got_out, pair_in, pair_out,
    term_in, term_out, back_in, back_out, ret_in, ret_out, place,
    ids, weights, tab_send, tab_got, tab, inv, inv_smem, slot_of_pair,
    rs_send, rs_got, kept, ag, rp,
    load_sem, tab_sem, tab_ss, tab_rs, fo_ss, fo_rs, fi_ss, fi_rs,
    bi_ss, bi_rs, bo_ss, bo_rs, rs_ss, rs_rs, ag_ss, ag_rs, rp_ss, rp_rs,
):
    me = lax.axis_index("adapter")
    mx, mz = me // SIDE, me % SIDE
    dp = lax.axis_index("dp")
    top = ids.shape[1]
    pairs = 2 * top
    width = top * RANK
    length = act.shape[1]
    chunk = length // HALF

    def there(off):
        return {"adapter": ((mx + off[0]) % SIDE) * SIDE + (mz + off[1]) % SIDE}

    def back(off):
        return {"adapter": ((mx + SIDE - off[0]) % SIDE) * SIDE + (mz + SIDE - off[1]) % SIDE}

    def beside(d):
        return {"dp": (dp + d) % DP}

    def push(src, dst, ss, rs, dev):
        c = pltpu.make_async_remote_copy(
            src_ref=src, dst_ref=dst, send_sem=ss, recv_sem=rs, device_id=dev, device_id_type=MESH
        )
        c.start()
        return c

    loads = []
    for i, (src, dst) in enumerate(((fo_hbm, fo), (fi_hbm, fi), (cot_hbm, cot), (act_hbm, act))):
        loads.append(pltpu.make_async_copy(src, dst, load_sem.at[i]))
    id_copies = [
        pltpu.make_async_copy(ids_hbm, ids, tab_sem.at[2]),
        pltpu.make_async_copy(weights_hbm, weights, tab_sem.at[3]),
    ]
    for c in id_copies:
        c.start()
    bar = pltpu.get_barrier_semaphore()
    for off in ORDER:
        pl.semaphore_signal(bar, inc=1, device_id=there(off), device_id_type=MESH)
    for d in range(1, DP):
        pl.semaphore_signal(bar, inc=1, device_id=beside(d), device_id_type=MESH)
    for c in loads:
        c.start()

    def turn_of(p):
        o = lax.shift_right_logical(ids[p // top, p % top], 5)
        return ((mx - lax.shift_right_logical(o, 2)) & 3) * SIDE + ((mz - o) & 3)

    row = lax.broadcasted_iota(I32, (OWNERS, LANES), 0)
    lane = lax.broadcasted_iota(I32, (OWNERS, LANES), 1)
    named = jnp.full((OWNERS, LANES), -1, I32)
    which = jnp.zeros((OWNERS, LANES), I32)
    held = jnp.zeros((OWNERS, LANES), I32)
    id_copies[0].wait()
    for p in range(pairs):
        mine = row == turn_of(p)
        hit = mine & (lane == held)
        named = jnp.where(hit, ids[p // top, p % top] & (EXP_DEV - 1), named)
        which = jnp.where(hit, p, which)
        held = jnp.where(mine, held + 1, held)
    tab_send[...] = named

    pl.semaphore_wait(bar, len(ORDER) + DP - 1)
    tabs = []
    for i, off in enumerate(ORDER):
        at = pl.ds(rot(off), 1)
        tabs.append(push(tab_send.at[at], tab_got.at[at], tab_ss.at[i], tab_rs.at[i], back(off)))
    tab_got[0:1] = named[0:1]
    inv[...] = which
    inv_copy = pltpu.make_async_copy(inv, inv_smem, tab_sem.at[1])
    inv_copy.start()

    def pick(src, dst, j, c, named_here):
        dst[j, c] = src[jnp.clip(named_here, 0, EXP_DEV - 1)]

    fos, fis = [], []
    loads[0].wait()
    for i, off in enumerate(ORDER_FO):
        j = rot(off)
        tabs[ORDER.index(off)].wait_recv()
        here = tab_got[j:j + 1]
        for c in range(CAP):
            pick(fo, send_out, j, c, here[0, c])
        fos.append(push(send_out.at[j], got_out.at[j], fo_ss.at[i], fo_rs.at[i], there(off)))
    tab_copy = pltpu.make_async_copy(tab_got, tab, tab_sem.at[0])
    tab_copy.start()
    tab_copy.wait()
    for c in range(CAP):
        pick(fo, got_out, 0, c, tab[0, c])
    loads[1].wait()
    for c in range(CAP):
        for i, off in enumerate(ORDER_FI):
            j = rot(off)
            pick(fi, send_in, j, c, tab[j, c])
            n = c * len(ORDER) + i
            fis.append(push(send_in.at[j, c], got_in.at[j, c], fi_ss.at[n], fi_rs.at[n], there(off)))
    for c in range(CAP):
        pick(fi, got_in, 0, c, tab[0, c])
    for c in tabs:
        c.wait_send()
    turns = []
    for p in range(pairs):
        nth = jnp.int32(0)
        t = turn_of(p)
        for q in turns:
            nth = nth + jnp.where(q == t, 1, 0)
        turns.append(t)
        slot_of_pair[p] = t * CAP + jnp.minimum(nth, CAP - 1)
    id_copies[1].wait()

    def project(step, rows, got, pair):
        for b in range(2):
            for k in range(top):
                p = b * top + k
                s = slot_of_pair[p]
                pair[p] = got[lax.shift_right_logical(s, 1), s & (CAP - 1)]
            part = lax.dot_general(
                rows[b], pair[b * top:(b + 1) * top].reshape(width, pair.shape[2]),
                (((1,), (1,)), ((), ())), preferred_element_type=F32,
            )
            for h in range(HALF):
                rs_send[step, b * HALF + h] = part[h * chunk:(h + 1) * chunk]

    def combine(step):
        cs = [
            push(rs_send.at[step, (dp + d) % DP], rs_got.at[step, d],
                 rs_ss.at[step, d], rs_rs.at[step, d], beside(d))
            for d in range(1, DP)
        ]
        total = rs_send[step, dp]
        for d in range(1, DP):
            cs[d - 1].wait()
            total = total + rs_got[step, d]
        return total

    group = lax.shift_right_logical(lax.broadcasted_iota(I32, (1, width), 1), 4)
    scale = jnp.zeros((1, width), F32)
    for k in range(top):
        scale = jnp.where(group == k, weights[dp // HALF, k], scale)

    def spread(step, total):
        ag[step, dp] = (total * scale).astype(BF)
        return [
            push(ag.at[step, dp], ag.at[step, dp], ag_ss.at[step, d], ag_rs.at[step, d], beside(d))
            for d in range(1, DP)
        ]

    def terms(step, rows, term):
        for b in range(2):
            w = ag[step, b * HALF:(b + 1) * HALF].reshape(length, width)
            for s in range(0, rows.shape[2], COLS):
                t = lax.dot_general(
                    w, rows[b, :, s:s + COLS], (((0,), (0,)), ((), ())), preferred_element_type=F32
                )
                term[b * top:(b + 1) * top, :, s:s + COLS] = t.astype(BF).reshape(top, RANK, COLS)

    loads[2].wait()
    loads[3].wait()
    inv_copy.wait()
    for c in fos:
        c.wait()
    project(0, cot, got_out, pair_out)
    pulled = combine(0)
    kept[...] = pulled
    for c in spread(0, pulled):
        c.wait()

    def give(order, term, out, ret, ss, rs, part, parts):
        n = term.shape[2] // parts
        at = pl.ds(part * n, n)
        cs = []
        for i, off in enumerate(order):
            j = rot(off)
            for c in range(CAP):
                out[j, c, :, at] = term[inv_smem[j, c], :, at]
            k = part * len(ORDER) + i
            cs.append(push(out.at[j, :, :, at], ret.at[j, :, :, at], ss.at[k], rs.at[k], back(off)))
        for c in range(CAP):
            ret[0, c, :, at] = term[inv_smem[0, c], :, at]
        return cs

    terms(0, act, term_in)
    bis = [give(ORDER_BI, term_in, back_in, ret_in, bi_ss, bi_rs, part, PARTS) for part in range(PARTS)]

    for c in fis:
        c.wait()
    project(1, act, got_in, pair_in)
    projected = combine(1)
    ags = spread(1, projected)
    rp[dp] = jnp.broadcast_to(jnp.sum(projected * kept[...], axis=0, keepdims=True), rp.shape[1:])
    rps = [push(rp.at[dp], rp.at[dp], rp_ss.at[d], rp_rs.at[d], beside(d)) for d in range(1, DP)]
    for c in ags:
        c.wait()
    terms(1, cot, term_out)
    bos = give(ORDER_BO, term_out, back_out, ret_out, bo_ss, bo_rs, 0, 1)

    for b in range(2):
        w = ag[0, b * HALF:(b + 1) * HALF].reshape(length, width)
        f = pair_in.at[b * top:(b + 1) * top]
        for s in range(0, fi.shape[2], COLS):
            ig[b, :, s:s + COLS] = jnp.dot(
                w, f[:, :, s:s + COLS].reshape(width, COLS), preferred_element_type=F32
            )
    for c in rps:
        c.wait()
    sums = jnp.concatenate(
        [jnp.sum(rp[b * HALF:(b + 1) * HALF], axis=0)[0:1] for b in range(2)]
        + [jnp.zeros((6, width), F32)], axis=0,
    )
    fold = jnp.where(
        lax.shift_right_logical(lax.broadcasted_iota(I32, (width, LANES), 0), 4)
        == lax.broadcasted_iota(I32, (width, LANES), 1), 1.0, 0.0,
    )
    router[...] = jnp.dot(
        sums, fold, precision=lax.Precision.HIGHEST, preferred_element_type=F32
    )[0:2, 0:top]

    total_rows = EXP_DEV * RANK
    slots = OWNERS * CAP
    spot = lax.broadcasted_iota(I32, (1, slots * RANK), 1)
    target = jnp.full((1, slots * RANK), -1, I32)
    for s in range(slots):
        e = tab[s // CAP, s % CAP]
        target = jnp.where(lax.shift_right_logical(spot, 4) == s, e * RANK + (spot & (RANK - 1)), target)
    for r in range(0, total_rows, LANES):
        at = lax.broadcasted_iota(I32, (LANES, slots * RANK), 0) + r
        place[r:r + LANES, :] = jnp.where(at == target, 1.0, 0.0).astype(BF)

    def settle(ret, grad, start, stop, step):
        for s in range(start, stop, step):
            total = jnp.dot(
                place[...], ret[:, :, :, s:s + step].reshape(slots * RANK, step), preferred_element_type=F32
            )
            grad[:, :, s:s + step] = total.astype(BF).reshape(EXP_DEV, RANK, step)

    ff = fi.shape[2]
    for part in range(PARTS):
        for c in bis[part]:
            c.wait()
        settle(ret_in, gi, part * ff // PARTS, (part + 1) * ff // PARTS, FINAL)
    for c in bos:
        c.wait()
    settle(ret_out, go, 0, fo.shape[2], 256)


def store_kernel(*refs):
    n = len(refs) // 2
    srcs, dsts, sem = refs[:n], refs[n:2 * n], refs[-1]
    copies = []
    for src, dst in zip(srcs, dsts):
        parts = SPLIT if src.shape[0] % SPLIT == 0 else 1
        step = src.shape[0] // parts
        for p in range(parts):
            at = pl.ds(p * step, step)
            copies.append(pltpu.make_async_copy(src.at[at], dst.at[at], sem.at[len(copies)]))
    for c in copies:
        c.start()
    for c in copies:
        c.wait()


def body(activations, cotangent, factor_in, factor_out, adapter_ids, router_weights):
    req, top = adapter_ids.shape
    tokens, ff = activations.shape
    model = cotangent.shape[1]
    length = tokens // req
    pairs = req * top
    chunk = tokens // DP
    width = top * RANK
    hbm = pl.BlockSpec(memory_space=pltpu.HBM)
    vmem = pl.BlockSpec(memory_space=pltpu.VMEM)
    dma = pltpu.SemaphoreType.DMA
    far = OWNERS - 1

    def slots(n):
        return pltpu.VMEM((OWNERS, CAP, RANK, n), BF)

    def by_pair(n):
        return pltpu.VMEM((pairs, RANK, n), BF)

    results = pl.pallas_call(
        exchange_kernel,
        out_shape=(
            pltpu.VMEM((req, length, ff), F32),
            pltpu.VMEM((EXP_DEV, RANK, ff), BF),
            pltpu.VMEM((EXP_DEV, RANK, model), BF),
            pltpu.VMEM((req, top), F32),
        ),
        in_specs=[hbm] * 6,
        out_specs=(vmem, vmem, vmem, vmem),
        scratch_shapes=[
            pltpu.VMEM((EXP_DEV, RANK, ff), BF),
            pltpu.VMEM((EXP_DEV, RANK, model), BF),
            pltpu.VMEM((req, length, ff), BF),
            pltpu.VMEM((req, length, model), BF),
            slots(ff), slots(model), slots(ff), slots(model),
            by_pair(ff), by_pair(model), by_pair(ff), by_pair(model),
            slots(ff), slots(model), slots(ff), slots(model),
            pltpu.VMEM((EXP_DEV * RANK, OWNERS * CAP * RANK), BF),
            pltpu.SMEM((req, top), I32),
            pltpu.SMEM((req, top), F32),
            pltpu.VMEM((OWNERS, LANES), I32),
            pltpu.VMEM((OWNERS, LANES), I32),
            pltpu.SMEM((OWNERS, LANES), I32),
            pltpu.VMEM((OWNERS, LANES), I32),
            pltpu.SMEM((OWNERS, LANES), I32),
            pltpu.SMEM((pairs,), I32),
            pltpu.VMEM((2, DP, chunk, width), F32),
            pltpu.VMEM((2, DP, chunk, width), F32),
            pltpu.VMEM((chunk, width), F32),
            pltpu.VMEM((2, DP, chunk, width), BF),
            pltpu.VMEM((DP, 8, width), F32),
            dma((4,)), dma((4,)),
            dma((far,)), dma((far,)),
            dma((far,)), dma((far,)),
            dma((CAP * far,)), dma((CAP * far,)),
            dma((PARTS * far,)), dma((PARTS * far,)),
            dma((far,)), dma((far,)),
            dma((2, DP)), dma((2, DP)), dma((2, DP)), dma((2, DP)), dma((DP,)), dma((DP,)),
        ],
        compiler_params=pltpu.CompilerParams(
            collective_id=0, has_side_effects=True, vmem_limit_bytes=44 << 20
        ),
        name="exchange",
    )(
        *(
            pltpu.with_memory_space_constraint(x, pltpu.HBM)
            for x in (
                adapter_ids, router_weights, factor_in, factor_out,
                activations.reshape(req, length, ff), cotangent.reshape(req, length, model),
            )
        ),
    )
    input_grad, grad_in, grad_out, router_grad = pl.pallas_call(
        store_kernel,
        out_shape=tuple(jax.ShapeDtypeStruct(r.shape, r.dtype) for r in results),
        in_specs=[vmem] * 4,
        out_specs=(hbm,) * 4,
        scratch_shapes=[dma((4 * SPLIT,))],
        compiler_params=pltpu.CompilerParams(vmem_limit_bytes=1 << 20),
        name="store",
    )(*(pltpu.with_memory_space_constraint(r, pltpu.VMEM) for r in results))
    return input_grad.reshape(tokens, ff), grad_in, grad_out, router_grad


def solution(mesh):
    return jax.shard_map(
        body,
        mesh=mesh,
        in_specs=(
            P("adapter", "dp"),
            P("adapter", "dp"),
            P("adapter", None, "dp"),
            P("adapter", None, "dp"),
            P("adapter", None),
            P("adapter", None),
        ),
        out_specs=(
            P("adapter", "dp"),
            P("adapter", None, "dp"),
            P("adapter", None, "dp"),
            P("adapter", None),
        ),
        check_vma=False,
    )
```

```python
import jax
import jax.numpy as jnp
from jax import lax
from jax.experimental import pallas as pl
from jax.experimental.pallas import tpu as pltpu
from jax.sharding import PartitionSpec as P

MESH = pl.DeviceIdType.MESH
SIDE = 4
OWNERS = SIDE * SIDE
CAP = 2
RANK = 16
EXP_DEV = 32
DP = 8
HALF = DP // 2
LANES = 128
COLS = 512
FINAL = 256
PARTS = 2
SPLIT = 1
ORDER = ((2, 0), (0, 2), (1, 0), (3, 0), (0, 1), (0, 3), (1, 1), (3, 3), (1, 3), (3, 1), (2, 1), (2, 3), (1, 2), (3, 2), (2, 2))
ORDER_FO = ((2, 0), (0, 2), (1, 0), (3, 0), (0, 1), (0, 3), (1, 1), (3, 3), (1, 3), (3, 1), (2, 1), (2, 3), (1, 2), (3, 2), (2, 2))
ORDER_FI = ((2, 0), (0, 2), (1, 0), (3, 0), (0, 1), (0, 3), (1, 1), (3, 3), (1, 3), (3, 1), (2, 1), (2, 3), (1, 2), (3, 2), (2, 2))
ORDER_BI = ((2, 0), (0, 2), (1, 0), (3, 0), (0, 1), (0, 3), (1, 1), (3, 3), (1, 3), (3, 1), (2, 1), (2, 3), (1, 2), (3, 2), (2, 2))
ORDER_BO = ((2, 2), (2, 1), (2, 3), (1, 2), (3, 2), (1, 1), (3, 3), (1, 3), (3, 1), (2, 0), (0, 2), (1, 0), (3, 0), (0, 1), (0, 3))
BF, F32, I32 = jnp.bfloat16, jnp.float32, jnp.int32


def rot(off):
    return off[0] * SIDE + off[1]


def exchange_kernel(
    ids_hbm, weights_hbm, fi_hbm, fo_hbm, act_hbm, cot_hbm,
    ig, gi, go, router,
    fi, fo, act, cot, send_in, send_out, got_in, got_out, pair_in, pair_out,
    term_in, term_out, back_in, back_out, ret_in, ret_out, place,
    ids, weights, tab_send, tab_got, tab, inv, inv_smem, slot_of_pair,
    rs_send, rs_got, kept, ag, rp,
    load_sem, tab_sem, tab_ss, tab_rs, fo_ss, fo_rs, fi_ss, fi_rs,
    bi_ss, bi_rs, bo_ss, bo_rs, rs_ss, rs_rs, ag_ss, ag_rs, rp_ss, rp_rs,
):
    me = lax.axis_index("adapter")
    mx, mz = me // SIDE, me % SIDE
    dp = lax.axis_index("dp")
    top = ids.shape[1]
    pairs = 2 * top
    width = top * RANK
    length = act.shape[1]
    chunk = length // HALF

    def there(off):
        return {"adapter": ((mx + off[0]) % SIDE) * SIDE + (mz + off[1]) % SIDE}

    def back(off):
        return {"adapter": ((mx + SIDE - off[0]) % SIDE) * SIDE + (mz + SIDE - off[1]) % SIDE}

    def beside(d):
        return {"dp": (dp + d) % DP}

    def push(src, dst, ss, rs, dev):
        c = pltpu.make_async_remote_copy(
            src_ref=src, dst_ref=dst, send_sem=ss, recv_sem=rs, device_id=dev, device_id_type=MESH
        )
        c.start()
        return c

    loads = []
    for i, (src, dst) in enumerate(((fo_hbm, fo), (fi_hbm, fi), (cot_hbm, cot), (act_hbm, act))):
        loads.append(pltpu.make_async_copy(src, dst, load_sem.at[i]))
    id_copies = [
        pltpu.make_async_copy(ids_hbm, ids, tab_sem.at[2]),
        pltpu.make_async_copy(weights_hbm, weights, tab_sem.at[3]),
    ]
    for c in id_copies:
        c.start()
    bar = pltpu.get_barrier_semaphore()
    for off in ORDER:
        pl.semaphore_signal(bar, inc=1, device_id=there(off), device_id_type=MESH)
    for d in range(1, DP):
        pl.semaphore_signal(bar, inc=1, device_id=beside(d), device_id_type=MESH)
    for c in loads:
        c.start()

    def turn_of(p):
        o = lax.shift_right_logical(ids[p // top, p % top], 5)
        return ((mx - lax.shift_right_logical(o, 2)) & 3) * SIDE + ((mz - o) & 3)

    row = lax.broadcasted_iota(I32, (OWNERS, LANES), 0)
    lane = lax.broadcasted_iota(I32, (OWNERS, LANES), 1)
    both = lane == CAP
    named = jnp.where(both, 0, -1)
    which = jnp.zeros((OWNERS, LANES), I32)
    held = jnp.zeros((OWNERS, LANES), I32)
    id_copies[0].wait()
    for p in range(pairs):
        mine = row == turn_of(p)
        hit = mine & (lane == held)
        e = ids[p // top, p % top] & (EXP_DEV - 1)
        named = jnp.where(hit, e, named)
        named = jnp.where(mine & both, named + jnp.where(held == 0, e, e * EXP_DEV), named)
        which = jnp.where(hit, p, which)
        held = jnp.where(mine, held + 1, held)
    tab_send[...] = named

    pl.semaphore_wait(bar, len(ORDER) + DP - 1)
    tabs = []
    for i, off in enumerate(ORDER):
        at = pl.ds(rot(off), 1)
        tabs.append(push(tab_send.at[at], tab_got.at[at], tab_ss.at[i], tab_rs.at[i], back(off)))
    tab_got[0:1] = named[0:1]
    inv[...] = which
    inv_copy = pltpu.make_async_copy(inv, inv_smem, tab_sem.at[1])
    inv_copy.start()

    def pick(src, dst, j, c, named_here):
        dst[j, c] = src[jnp.clip(named_here, 0, EXP_DEV - 1)]

    fos, fis = [], []
    loads[0].wait()
    for i, off in enumerate(ORDER_FO):
        j = rot(off)
        tabs[ORDER.index(off)].wait_recv()
        here = tab_got[j:j + 1]
        pair = here[0, CAP]
        pick(fo, send_out, j, 0, pair & (EXP_DEV - 1))
        pick(fo, send_out, j, 1, lax.shift_right_logical(pair, 5) & (EXP_DEV - 1))
        fos.append(push(send_out.at[j], got_out.at[j], fo_ss.at[i], fo_rs.at[i], there(off)))
    tab_copy = pltpu.make_async_copy(tab_got, tab, tab_sem.at[0])
    tab_copy.start()
    tab_copy.wait()
    for c in range(CAP):
        pick(fo, got_out, 0, c, tab[0, c])
    loads[1].wait()
    for c in range(CAP):
        for i, off in enumerate(ORDER_FI):
            j = rot(off)
            pick(fi, send_in, j, c, tab[j, c])
            n = c * len(ORDER) + i
            fis.append(push(send_in.at[j, c], got_in.at[j, c], fi_ss.at[n], fi_rs.at[n], there(off)))
    for c in range(CAP):
        pick(fi, got_in, 0, c, tab[0, c])
    for c in tabs:
        c.wait_send()
    turns = []
    for p in range(pairs):
        nth = jnp.int32(0)
        t = turn_of(p)
        for q in turns:
            nth = nth + jnp.where(q == t, 1, 0)
        turns.append(t)
        slot_of_pair[p] = t * CAP + jnp.minimum(nth, CAP - 1)
    id_copies[1].wait()

    def project(step, rows, got, pair):
        for b in range(2):
            for k in range(top):
                p = b * top + k
                s = slot_of_pair[p]
                pair[p] = got[lax.shift_right_logical(s, 1), s & (CAP - 1)]
            part = lax.dot_general(
                rows[b], pair[b * top:(b + 1) * top].reshape(width, pair.shape[2]),
                (((1,), (1,)), ((), ())), preferred_element_type=F32,
            )
            for h in range(HALF):
                rs_send[step, b * HALF + h] = part[h * chunk:(h + 1) * chunk]

    def combine(step):
        cs = [
            push(rs_send.at[step, (dp + d) % DP], rs_got.at[step, d],
                 rs_ss.at[step, d], rs_rs.at[step, d], beside(d))
            for d in range(1, DP)
        ]
        total = rs_send[step, dp]
        for d in range(1, DP):
            cs[d - 1].wait()
            total = total + rs_got[step, d]
        return total

    group = lax.shift_right_logical(lax.broadcasted_iota(I32, (1, width), 1), 4)
    scale = jnp.zeros((1, width), F32)
    for k in range(top):
        scale = jnp.where(group == k, weights[dp // HALF, k], scale)

    def spread(step, total):
        ag[step, dp] = (total * scale).astype(BF)
        return [
            push(ag.at[step, dp], ag.at[step, dp], ag_ss.at[step, d], ag_rs.at[step, d], beside(d))
            for d in range(1, DP)
        ]

    def terms(step, rows, term):
        for b in range(2):
            w = ag[step, b * HALF:(b + 1) * HALF].reshape(length, width)
            for s in range(0, rows.shape[2], COLS):
                t = lax.dot_general(
                    w, rows[b, :, s:s + COLS], (((0,), (0,)), ((), ())), preferred_element_type=F32
                )
                term[b * top:(b + 1) * top, :, s:s + COLS] = t.astype(BF).reshape(top, RANK, COLS)

    loads[2].wait()
    loads[3].wait()
    inv_copy.wait()
    for c in fos:
        c.wait()
    project(0, cot, got_out, pair_out)
    pulled = combine(0)
    kept[...] = pulled
    for c in spread(0, pulled):
        c.wait()

    def give(order, term, out, ret, ss, rs, part, parts):
        n = term.shape[2] // parts
        at = pl.ds(part * n, n)
        cs = []
        for i, off in enumerate(order):
            j = rot(off)
            for c in range(CAP):
                out[j, c, :, at] = term[inv_smem[j, c], :, at]
            k = part * len(ORDER) + i
            cs.append(push(out.at[j, :, :, at], ret.at[j, :, :, at], ss.at[k], rs.at[k], back(off)))
        for c in range(CAP):
            ret[0, c, :, at] = term[inv_smem[0, c], :, at]
        return cs

    terms(0, act, term_in)
    bis = [give(ORDER_BI, term_in, back_in, ret_in, bi_ss, bi_rs, part, PARTS) for part in range(PARTS)]

    for c in fis:
        c.wait()
    project(1, act, got_in, pair_in)
    projected = combine(1)
    ags = spread(1, projected)
    rp[dp] = jnp.broadcast_to(jnp.sum(projected * kept[...], axis=0, keepdims=True), rp.shape[1:])
    rps = [push(rp.at[dp], rp.at[dp], rp_ss.at[d], rp_rs.at[d], beside(d)) for d in range(1, DP)]
    for c in ags:
        c.wait()
    terms(1, cot, term_out)
    bos = give(ORDER_BO, term_out, back_out, ret_out, bo_ss, bo_rs, 0, 1)

    for b in range(2):
        w = ag[0, b * HALF:(b + 1) * HALF].reshape(length, width)
        f = pair_in.at[b * top:(b + 1) * top]
        for s in range(0, fi.shape[2], COLS):
            ig[b, :, s:s + COLS] = jnp.dot(
                w, f[:, :, s:s + COLS].reshape(width, COLS), preferred_element_type=F32
            )
    for c in rps:
        c.wait()
    sums = jnp.concatenate(
        [jnp.sum(rp[b * HALF:(b + 1) * HALF], axis=0)[0:1] for b in range(2)]
        + [jnp.zeros((6, width), F32)], axis=0,
    )
    fold = jnp.where(
        lax.shift_right_logical(lax.broadcasted_iota(I32, (width, LANES), 0), 4)
        == lax.broadcasted_iota(I32, (width, LANES), 1), 1.0, 0.0,
    )
    router[...] = jnp.dot(
        sums, fold, precision=lax.Precision.HIGHEST, preferred_element_type=F32
    )[0:2, 0:top]

    total_rows = EXP_DEV * RANK
    slots = OWNERS * CAP
    spot = lax.broadcasted_iota(I32, (1, slots * RANK), 1)
    target = jnp.full((1, slots * RANK), -1, I32)
    for s in range(slots):
        e = tab[s // CAP, s % CAP]
        target = jnp.where(lax.shift_right_logical(spot, 4) == s, e * RANK + (spot & (RANK - 1)), target)
    for r in range(0, total_rows, LANES):
        at = lax.broadcasted_iota(I32, (LANES, slots * RANK), 0) + r
        place[r:r + LANES, :] = jnp.where(at == target, 1.0, 0.0).astype(BF)

    def settle(ret, grad, start, stop, step):
        for s in range(start, stop, step):
            total = jnp.dot(
                place[...], ret[:, :, :, s:s + step].reshape(slots * RANK, step), preferred_element_type=F32
            )
            grad[:, :, s:s + step] = total.astype(BF).reshape(EXP_DEV, RANK, step)

    ff = fi.shape[2]
    for part in range(PARTS):
        for c in bis[part]:
            c.wait()
        settle(ret_in, gi, part * ff // PARTS, (part + 1) * ff // PARTS, FINAL)
    for c in bos:
        c.wait()
    settle(ret_out, go, 0, fo.shape[2], 256)


def store_kernel(*refs):
    n = len(refs) // 2
    srcs, dsts, sem = refs[:n], refs[n:2 * n], refs[-1]
    copies = []
    for src, dst in zip(srcs, dsts):
        parts = SPLIT if src.shape[0] % SPLIT == 0 else 1
        step = src.shape[0] // parts
        for p in range(parts):
            at = pl.ds(p * step, step)
            copies.append(pltpu.make_async_copy(src.at[at], dst.at[at], sem.at[len(copies)]))
    for c in copies:
        c.start()
    for c in copies:
        c.wait()


def body(activations, cotangent, factor_in, factor_out, adapter_ids, router_weights):
    req, top = adapter_ids.shape
    tokens, ff = activations.shape
    model = cotangent.shape[1]
    length = tokens // req
    pairs = req * top
    chunk = tokens // DP
    width = top * RANK
    hbm = pl.BlockSpec(memory_space=pltpu.HBM)
    vmem = pl.BlockSpec(memory_space=pltpu.VMEM)
    dma = pltpu.SemaphoreType.DMA
    far = OWNERS - 1

    def slots(n):
        return pltpu.VMEM((OWNERS, CAP, RANK, n), BF)

    def by_pair(n):
        return pltpu.VMEM((pairs, RANK, n), BF)

    results = pl.pallas_call(
        exchange_kernel,
        out_shape=(
            pltpu.VMEM((req, length, ff), F32),
            pltpu.VMEM((EXP_DEV, RANK, ff), BF),
            pltpu.VMEM((EXP_DEV, RANK, model), BF),
            pltpu.VMEM((req, top), F32),
        ),
        in_specs=[hbm] * 6,
        out_specs=(vmem, vmem, vmem, vmem),
        scratch_shapes=[
            pltpu.VMEM((EXP_DEV, RANK, ff), BF),
            pltpu.VMEM((EXP_DEV, RANK, model), BF),
            pltpu.VMEM((req, length, ff), BF),
            pltpu.VMEM((req, length, model), BF),
            slots(ff), slots(model), slots(ff), slots(model),
            by_pair(ff), by_pair(model), by_pair(ff), by_pair(model),
            slots(ff), slots(model), slots(ff), slots(model),
            pltpu.VMEM((EXP_DEV * RANK, OWNERS * CAP * RANK), BF),
            pltpu.SMEM((req, top), I32),
            pltpu.SMEM((req, top), F32),
            pltpu.VMEM((OWNERS, LANES), I32),
            pltpu.VMEM((OWNERS, LANES), I32),
            pltpu.SMEM((OWNERS, LANES), I32),
            pltpu.VMEM((OWNERS, LANES), I32),
            pltpu.SMEM((OWNERS, LANES), I32),
            pltpu.SMEM((pairs,), I32),
            pltpu.VMEM((2, DP, chunk, width), F32),
            pltpu.VMEM((2, DP, chunk, width), F32),
            pltpu.VMEM((chunk, width), F32),
            pltpu.VMEM((2, DP, chunk, width), BF),
            pltpu.VMEM((DP, 8, width), F32),
            dma((4,)), dma((4,)),
            dma((far,)), dma((far,)),
            dma((far,)), dma((far,)),
            dma((CAP * far,)), dma((CAP * far,)),
            dma((PARTS * far,)), dma((PARTS * far,)),
            dma((far,)), dma((far,)),
            dma((2, DP)), dma((2, DP)), dma((2, DP)), dma((2, DP)), dma((DP,)), dma((DP,)),
        ],
        compiler_params=pltpu.CompilerParams(
            collective_id=0, has_side_effects=True, vmem_limit_bytes=44 << 20
        ),
        name="exchange",
    )(
        *(
            pltpu.with_memory_space_constraint(x, pltpu.HBM)
            for x in (
                adapter_ids, router_weights, factor_in, factor_out,
                activations.reshape(req, length, ff), cotangent.reshape(req, length, model),
            )
        ),
    )
    input_grad, grad_in, grad_out, router_grad = pl.pallas_call(
        store_kernel,
        out_shape=tuple(jax.ShapeDtypeStruct(r.shape, r.dtype) for r in results),
        in_specs=[vmem] * 4,
        out_specs=(hbm,) * 4,
        scratch_shapes=[dma((4 * SPLIT,))],
        compiler_params=pltpu.CompilerParams(vmem_limit_bytes=1 << 20),
        name="store",
    )(*(pltpu.with_memory_space_constraint(r, pltpu.VMEM) for r in results))
    return input_grad.reshape(tokens, ff), grad_in, grad_out, router_grad


def solution(mesh):
    return jax.shard_map(
        body,
        mesh=mesh,
        in_specs=(
            P("adapter", "dp"),
            P("adapter", "dp"),
            P("adapter", None, "dp"),
            P("adapter", None, "dp"),
            P("adapter", None),
            P("adapter", None),
        ),
        out_specs=(
            P("adapter", "dp"),
            P("adapter", None, "dp"),
            P("adapter", None, "dp"),
            P("adapter", None),
        ),
        check_vma=False,
    )
```
